128 devices in a mesh: blk: 16 (over x_hi, z, core), user: 8 (over y, x_lo).
Axes of the slice: x: 4 (x_hi: 2, x_lo: 2; x = x_hi * 2 + x_lo), y: 4, z: 4, core: 2. Of those that a mesh axis runs over, the one named last changes fastest.
Arguments:
- user_factors: float32 [524288, 256], P(('blk', 'user')), may hold values from -2 to 2
- item_factors: float32 [16384, 256], P(('blk', 'user')), may hold values from -2 to 2
- block_index: int32 [3, 1024, 2, 4], P(None, ('blk', 'user')), may hold values from 0 to 15, as said below
- block_count: int32 [3, 1024, 2], P(None, ('blk', 'user')), may hold values from 1 to 4
- ratings: int32 [3, 1024, 2, 4, 128, 128], P(None, ('blk', 'user')), may hold values from 0 to 10
Outputs:
- users_out: float32 [524288, 256], P(('blk', 'user'))
- items_out: float32 [16384, 256], P(('blk', 'user'))
The draws below stay inside these ranges and needn't reach their ends.
Inputs may be any that keep to these rules, and one draw needn't show every extreme that they name: `block_index`: the 4 block numbers of one tile are distinct.
All inputs are finite; a program needn't handle non-finite values.
Results may differ from the reference program's by a relative error of at most 0.0003.
Values sent between devices are 32-bit elements; how exact they have to be, the bound alone decides.
A program may use at most 128 MiB of HBM per device.

```python
import jax
import jax.numpy as jnp
from jax import lax

R = 256
BL = 128
SUB = 4
OCC = 4
TR = 8
TC = 2
STEPS = 3
TROWS = 1024
USERS = 524288
ITEMS = 16384
N_BLK = 16
N_USER = 8


def draw_block_index(key, part):
    tiles = SUB * SUB
    scores = jax.random.randint(key, (STEPS, TROWS, TC, tiles), 0, 1 << 20)
    values = jnp.arange(tiles, dtype=jnp.int32)
    scores = scores * tiles + values
    first = (jnp.arange(STEPS)[:, None, None, None] == 0) & (jnp.arange(TROWS)[None, :, None, None] == 0) & (jnp.arange(TC)[None, None, :, None] == 0)
    forced = jnp.where(values == tiles - 1, -2, jnp.where(values == 0, -1, scores))
    scores = jnp.where(first, forced, scores)
    order = jnp.argsort(scores, axis=-1, stable=True)
    return order[..., :OCC].astype(jnp.int32)


def draw_block_count(key, part):
    level_key = jax.random.fold_in(key, 11)
    count_key = jax.random.fold_in(key, 23)
    level = jax.random.randint(level_key, (STEPS, TROWS, 1), 1, OCC + 1)
    counts = jax.random.randint(count_key, (STEPS, TROWS, TC), 1, level + 1)
    first = (jnp.arange(STEPS)[:, None, None] == 0) & (jnp.arange(TROWS)[None, :, None] == 0) & (jnp.arange(TC)[None, None, :] == 0)
    return jnp.where(first, OCC, counts).astype(jnp.int32)


def with_ends(array, rng, least, high):
    longest = array.shape.index(max(array.shape))
    spots = []
    for shift in (0, 1):
        where = [jax.random.randint(jax.random.fold_in(rng, axis), (), 0, length) for axis, length in enumerate(array.shape)]
        where[longest] = (where[longest] + shift) % array.shape[longest]
        spots.append(tuple(where))
    return array.at[spots[0]].set(least).at[spots[1]].set(high)


def block_levels(own_key, extent, shards, smallest, top_value):
    level, own = 1.0, jax.random.fold_in(own_key, 6)
    for axis_at, blocks in shards:
        draws = jnp.exp(jax.random.uniform(jax.random.fold_in(own, axis_at), (blocks,), jnp.float32, smallest / len(shards), top_value / len(shards)))
        level = level * jnp.repeat(draws, extent[axis_at] // blocks).reshape([-1 if axis == axis_at else 1 for axis in range(len(extent))])
    return level


def gaussian(stream_key, shape, deviation, most, split=(), kind=jnp.bfloat16):
    entries = deviation * jax.random.normal(stream_key, shape, jnp.float32)
    if split:
        entries = entries * block_levels(stream_key, shape, split, -0.22, 0.18)
    return jnp.clip(entries, -most, most).astype(kind)


def setup_inputs(seed: int = 0) -> dict:
    key_list = jax.random.split(jax.random.key(seed), 6)
    return {
        "user_factors": gaussian(key_list[0], (USERS, R), 0.3, 2.0, ((0, 128),), jnp.float32),
        "item_factors": gaussian(key_list[1], (ITEMS, R), 0.3, 2.0, ((0, 128),), jnp.float32),
        "block_index": draw_block_index(jax.random.fold_in(key_list[5], 71), 0),
        "block_count": draw_block_count(jax.random.fold_in(key_list[5], 71), 0),
        "ratings": with_ends(jax.random.randint(key_list[4], (STEPS, TROWS, TC, OCC, BL, BL), 0, 11), jax.random.fold_in(key_list[4], 1), 0, 10).astype(jnp.int32),
    }


user_rate = 0.01
item_rate = 0.0015
decay_rate = 0.05


def local_grads(user_rows, item_group, tile_index, tile_count, tile_ratings):
    tile_rows = tile_index.shape[0]
    tile_cols = tile_index.shape[1]
    slots = tile_index.shape[2]
    rank = user_rows.shape[1]
    block = tile_ratings.shape[-1]
    parts = user_rows.shape[0] // (tile_rows * block)
    sub_row = tile_index // parts
    sub_col = tile_index % parts
    user_tiles = user_rows.reshape(tile_rows, parts, block, rank)
    item_tiles = item_group.reshape(tile_cols, parts, block, rank)
    row_ids = jnp.arange(tile_rows)[:, None, None]
    col_ids = jnp.arange(tile_cols)[None, :, None]
    user_blocks = user_tiles[row_ids, sub_row]
    item_blocks = item_tiles[col_ids, sub_col]
    predicted = jnp.einsum('abkir,abkjr->abkij', user_blocks, item_blocks, precision=lax.Precision.HIGHEST)
    slot_ids = jnp.arange(slots)[None, None, :, None, None]
    observed = (tile_ratings > 0) & (slot_ids < tile_count[:, :, None, None, None])
    residuals = jnp.where(observed, 0.5 * tile_ratings.astype(jnp.float32) - predicted, 0.0)
    user_terms = jnp.einsum('abkij,abkjr->abkir', residuals, item_blocks, precision=lax.Precision.HIGHEST)
    item_terms = jnp.einsum('abkij,abkir->abkjr', residuals, user_blocks, precision=lax.Precision.HIGHEST)
    part_ids = jnp.arange(parts)
    row_hot = (sub_row[..., None] == part_ids).astype(jnp.float32)
    col_hot = (sub_col[..., None] == part_ids).astype(jnp.float32)
    grad_users = jnp.einsum('abko,abkir->aoir', row_hot, user_terms, precision=lax.Precision.HIGHEST)
    grad_items = jnp.einsum('abko,abkjr->bojr', col_hot, item_terms, precision=lax.Precision.HIGHEST)
    return grad_users.reshape(user_rows.shape), grad_items.reshape(item_group.shape)


def reference(user_factors, item_factors, block_index, block_count, ratings):
    user_rows = user_factors
    item_rows = item_factors
    spans = N_BLK * N_USER
    group_len = TC * SUB * BL
    user_len = TR * SUB * BL
    for step in range(STEPS):
        index_step = block_index[step].reshape(spans, TR, TC, OCC)
        count_step = block_count[step].reshape(spans, TR, TC)
        rating_step = ratings[step].reshape(spans, TR, TC, OCC, BL, BL)

        def visit(grad_items, inputs):
            span, user_span, tile_index, tile_count, tile_ratings = inputs
            source = ((span // N_USER - step) % N_BLK).astype(jnp.int32)
            start = (source * group_len).astype(jnp.int32)
            item_group = lax.dynamic_slice_in_dim(item_rows, start, group_len, 0)
            grad_u, grad_v = local_grads(user_span, item_group, tile_index, tile_count, tile_ratings)
            before = lax.dynamic_slice_in_dim(grad_items, start, group_len, 0)
            grad_items = lax.dynamic_update_slice_in_dim(grad_items, before + grad_v, start, 0)
            return grad_items, grad_u

        inputs = (jnp.arange(spans, dtype=jnp.int32), user_rows.reshape(spans, user_len, R), index_step, count_step, rating_step)
        grad_items, grad_users = lax.scan(visit, jnp.zeros(item_rows.shape, jnp.float32), inputs)
        grad_users = grad_users.reshape(user_rows.shape)
        user_rows = user_rows + user_rate * (grad_users - decay_rate * user_rows)
        item_rows = item_rows + item_rate * (grad_items - decay_rate * item_rows)
    rolled = jnp.roll(item_rows.reshape(N_BLK, group_len, R), STEPS, axis=0).reshape(item_rows.shape)
    return user_rows, rolled
```

```python
import functools

import jax
import jax.numpy as jnp
from jax import lax
from jax.experimental import pallas as pl
from jax.experimental.pallas import tpu as pltpu
from jax.sharding import PartitionSpec as P

STEPS = 3
USER_RATE = 0.01
ITEM_RATE = 0.0015
DECAY = 0.05
MESH = pl.DeviceIdType.MESH
F32 = jnp.float32
BF16 = jnp.bfloat16
RING = 8
VMEM_LIMIT = 16 << 20
COPY_IN = False


def split(x):
    hi = x.astype(BF16)
    return hi, (x - hi.astype(F32)).astype(BF16)


def chip_array(shape, dtype):
    return pltpu.VMEM(shape, dtype)


def on_chip(x):
    return pltpu.with_memory_space_constraint(x, pltpu.VMEM)


def off_chip(x):
    return pltpu.with_memory_space_constraint(x, pltpu.HBM)


def matmul(a, b, dims=((1,), (0,))):
    return lax.dot_general(a, b, (dims, ((), ())), preferred_element_type=F32)


def grads_kernel(step, idx, cnt, uhl, vhl, ubase, ratings, unew, gv, *refs):
    final, out_sems = (refs[0], refs[-1]) if step == STEPS - 1 else (None, None)
    rbuf, sems = refs[1:3] if step == STEPS - 1 else refs
    rows, cols = cnt.shape[1], cnt.shape[2]
    tiles = rows * cols
    side = rbuf.shape[1]
    sub = uhl.shape[0] // rows

    def place(tile):
        tile = jnp.minimum(tile, tiles - 1)
        return tile // cols, tile % cols

    def following(tile, slot):
        t, c = place(tile)
        last = slot + 1 >= cnt[step, t, c]
        return jnp.where(last, tile + 1, tile), jnp.where(last, 0, slot + 1)

    total = 0
    for t in range(rows):
        for c in range(cols):
            total = total + cnt[step, t, c]
    pairs = (total + 1) // 2

    def fetch(tile, slot, pos):
        t, c = place(tile)
        return pltpu.make_async_copy(ratings.at[step, t, c, slot], rbuf.at[pos], sems.at[pos])

    def fetch_pair(pair, cursor):
        for half in range(2):
            fetch(*cursor, lax.rem(2 * pair, RING) + half).start()
            cursor = following(*cursor)
        return cursor

    ahead = RING // 2 - 1
    cursor = (jnp.int32(0), jnp.int32(0))
    for pair in range(ahead):
        cursor = lax.cond(pair < pairs, functools.partial(fetch_pair, pair), lambda at: at, cursor)
    gv[...] = jnp.zeros_like(gv)
    if COPY_IN:
        unew[...] = ubase[...]

    def put(row):
        part = pl.ds(row * sub, sub)
        return pltpu.make_async_copy(unew.at[part], final.at[part], out_sems.at[row])

    def front(tile, slot, pos, floor):
        t, c = place(tile)
        q = idx[step, t, c, slot]
        row, item = t * sub + q // sub, c * sub + q % sub
        parts = matmul(uhl[row], vhl[item], ((1,), (1,)))
        predicted = parts[:side, :side] + (parts[:side, side:] + parts[side:, :side])
        rating = rbuf[pos]
        return row, item, jnp.where(rating > floor, 0.5 * rating.astype(F32) - predicted, 0.0)

    def back(row, item, residual):
        hi, lo = split(residual)
        both = jnp.concatenate([hi, hi], axis=1)
        user_term = matmul(both, vhl[item]) + matmul(lo, vhl[item, :side])
        hi, lo = split(residual.T)
        both = jnp.concatenate([hi, hi], axis=1)
        item_term = matmul(both, uhl[row]) + matmul(lo, uhl[row, :side])
        unew[row] += USER_RATE * user_term
        gv[item] += item_term

    def body(pair, carry):
        here, cursor = carry[:2], carry[2:]
        cursor = lax.cond(
            pair + ahead < pairs, functools.partial(fetch_pair, pair + ahead), lambda at: at, cursor
        )
        pos = lax.rem(2 * pair, RING)
        fetch(0, 0, pos).wait()
        fetch(0, 0, pos + 1).wait()
        second = following(*here)
        floor = jnp.where(2 * pair + 1 < total, 0, 1 << 20)
        first_out = front(*here, pos, 0)
        second_out = front(*second, pos + 1, floor)
        back(*first_out)
        back(*second_out)
        after = following(*second)
        if final is not None:
            row = here[0] // cols

            @pl.when((after[0] // cols > row) | (pair == pairs - 1))
            def _():
                put(row).start()

        return (*after, *cursor)

    lax.fori_loop(0, pairs, body, (jnp.int32(0), jnp.int32(0), *cursor))
    if final is not None:
        for row in range(rows):
            put(row).wait()


def local_grads(step, idx, cnt, uhl, vhl, ubase, ratings):
    side = ratings.shape[-1]
    rank = ubase.shape[-1]
    vmem = pl.BlockSpec(memory_space=pltpu.VMEM)
    smem = pl.BlockSpec(memory_space=pltpu.SMEM)
    outs = [chip_array(ubase.shape, F32), chip_array((vhl.shape[0], side, rank), F32)]
    out_specs = [vmem, vmem]
    scratch = [pltpu.VMEM((RING, side, side), jnp.int32), pltpu.SemaphoreType.DMA((RING,))]
    if step == STEPS - 1:
        outs.append(jax.ShapeDtypeStruct(ubase.shape, F32))
        out_specs.append(pl.BlockSpec(memory_space=pl.ANY))
        scratch.append(pltpu.SemaphoreType.DMA((cnt.shape[1],)))
    return pl.pallas_call(
        functools.partial(grads_kernel, step),
        out_shape=tuple(outs),
        in_specs=[smem, smem, vmem, vmem, vmem, pl.BlockSpec(memory_space=pl.ANY)],
        out_specs=tuple(out_specs),
        scratch_shapes=scratch,
        input_output_aliases={4: 0},
        compiler_params=pltpu.CompilerParams(vmem_limit_bytes=VMEM_LIMIT),
        name=f"grads{step}",
    )(idx, cnt, on_chip(uhl), on_chip(vhl), on_chip(ubase), off_chip(ratings))


class Links:
    def __init__(self, sends, recvs):
        self.sends, self.recvs = sends, recvs
        self.started = []
        self.count = 0

    def message(self):
        self.count += 1
        return self.count - 1

    def copy(self, number, src, dst, device):
        return pltpu.make_async_remote_copy(
            src_ref=src,
            dst_ref=dst,
            send_sem=self.sends.at[number],
            recv_sem=self.recvs.at[number],
            device_id=device,
            device_id_type=MESH,
        )

    def send(self, number, src, dst, device):
        copy = self.copy(number, src, dst, device)
        copy.start()
        self.started.append(copy)

    def arrived(self, number, dst, device):
        self.copy(number, dst, dst, device).wait_recv()


def exchange_kernel(reduce, gather, users, *refs):
    refs = list(refs)
    gv = refs.pop(0) if reduce else None
    vin = refs.pop(0)
    uin = refs.pop(0) if users else None
    vout = refs.pop(0) if reduce else None
    vhl = refs.pop(0) if gather else None
    uhl, ubase = (refs.pop(0), refs.pop(0)) if users else (None, None)
    if reduce:
        opp, stage, rin, xio, vnew = (refs.pop(0) for _ in range(5))
    if gather:
        vx, vy, vo = (refs.pop(0) for _ in range(3))
    uraw, load_sems = (refs.pop(0), refs.pop(0)) if users and not reduce else (None, None)
    sends, recvs = refs

    if uraw is not None:
        parts = uin.shape[0] // LOADS
        loads = [
            pltpu.make_async_copy(
                uin.at[pl.ds(i * parts, parts)], uraw.at[pl.ds(i * parts, parts)], load_sems.at[i]
            )
            for i in range(LOADS)
        ]
        for load in loads:
            load.start()
        uin = uraw
    else:
        loads = []

    blk, user = lax.axis_index("blk"), lax.axis_index("user")
    blks = lax.axis_size("blk")
    y, xl = user // 2, lax.rem(user, 2)
    ys = lax.axis_size("user") // 2
    up, down, across = lax.rem(y + 1, ys), lax.rem(y + ys - 1, ys), lax.rem(y + 2, ys)
    to_y = ((blk, up * 2 + xl), (blk, down * 2 + xl))
    from_y = (to_y[1], to_y[0])
    to_x = (blk, y * 2 + 1 - xl)
    after = (lax.rem(blk + 1, blks), user)
    before = (lax.rem(blk + blks - 1, blks), user)

    def number(row, which):
        return row * 2 + (1 - xl if which == 0 else xl)

    side = vin.shape[0]
    half = side // 2
    rows = (pl.ds(0, half), pl.ds(half, half))
    links = Links(sends, recvs)

    todo = [0]
    if users:
        blocks = uin.shape[0]

        def user_work(amount):
            start = todo[0]
            stop = min(blocks, start + amount)
            todo[0] = stop
            if start == stop:
                return
            while loads and (LOADS - len(loads)) * (blocks // LOADS) < stop:
                loads.pop(0).wait()

            def one(i, carry):
                x = uin[i]
                hi, lo = split(x)
                uhl[i, :side] = hi
                uhl[i, side:] = lo
                ubase[i] = x * (1.0 - USER_RATE * DECAY)
                return carry

            lax.fori_loop(start, stop, one, 0)
    else:

        def user_work(amount):
            pass

    barrier = pltpu.get_barrier_semaphore()
    greet = [to_y[0], to_y[1], to_x] + ([before] if reduce else [])
    for device in greet:
        pl.semaphore_signal(barrier, inc=1, device_id=device, device_id_type=MESH)
    pl.semaphore_wait(barrier, len(greet))

    if reduce:
        ids = {}
        for kind in "ABC":
            for d in range(2):
                for w in range(2):
                    ids[kind, d, w] = links.message()
        for w in range(2):
            for d in range(2):
                links.send(ids["A", d, w], gv.at[number(across, w), rows[d]], opp.at[d, w], to_y[d])
            for d in range(2):
                near = up if d == 0 else down
                links.send(
                    ids["B", d, w], gv.at[number(near, w), rows[1 - d]], rin.at[d, w, rows[1 - d]], to_y[d]
                )
        user_work(6)
        xids = [links.message() for _ in range(2)]
        for w in range(2):
            for d in range(2):
                near = up if d == 0 else down
                links.arrived(ids["A", d, w], opp.at[d, w], from_y[d])
                stage[d, w] = gv[number(near, w), rows[d]] + opp[d, w]
                links.send(ids["C", d, w], stage.at[d, w], rin.at[d, w, rows[d]], to_y[d])
            if w == 0:
                user_work(4)
        for h in range(2):
            links.arrived(ids["B", 1 - h, 0], rin.at[1 - h, 0, rows[h]], from_y[1 - h])
            links.arrived(ids["C", h, 0], rin.at[h, 0, rows[h]], from_y[h])
            xio[0, rows[h]] = gv[number(y, 0), rows[h]] + (rin[0, 0, rows[h]] + rin[1, 0, rows[h]])
            links.send(xids[h], xio.at[0, rows[h]], xio.at[1, rows[h]], to_x)
        user_work(8)
        nids = [links.message() for _ in range(2)]
        for h in range(2):
            links.arrived(ids["B", 1 - h, 1], rin.at[1 - h, 1, rows[h]], from_y[1 - h])
            links.arrived(ids["C", h, 1], rin.at[h, 1, rows[h]], from_y[h])
            links.arrived(xids[h], xio.at[1, rows[h]], to_x)
            grad = (gv[number(y, 1), rows[h]] + (rin[0, 1, rows[h]] + rin[1, 1, rows[h]])) + xio[1, rows[h]]
            old = vin[rows[h]]
            vnew[0, rows[h]] = old + ITEM_RATE * (grad - DECAY * old)
            links.send(nids[h], vnew.at[0, rows[h]], vnew.at[1, rows[h]], after)

    if gather:
        own = vnew.at[1] if reduce else vin
        gx = [links.message() for _ in range(2)]
        gy = {(d, w, h): links.message() for d in range(2) for w in range(2) for h in range(2)}
        gf = {(d, w): links.message() for d in range(2) for w in range(2)}

        def divide(block, h, ref):
            hi, lo = split(ref[rows[h]])
            vhl[block, rows[h]] = hi
            vhl[block, pl.ds(side + h * half, half)] = lo

        for h in range(2):
            if reduce:
                links.arrived(nids[h], vnew.at[1, rows[h]], before)
            links.send(gx[h], own.at[rows[h]], vx.at[rows[h]], to_x)
            for d in (h, 1 - h):
                links.send(gy[d, 1, h], own.at[rows[h]], vy.at[d, 1, rows[h]], to_y[d])
        for h in range(2):
            divide(user, h, own)
        user_work(4)
        for h in range(2):
            links.arrived(gx[h], vx.at[rows[h]], to_x)
            for d in (h, 1 - h):
                links.send(gy[d, 0, h], vx.at[rows[h]], vy.at[d, 0, rows[h]], to_y[d])
        for w in (1, 0):
            for d in range(2):
                links.arrived(gy[d, w, d], vy.at[d, w, rows[d]], from_y[d])
                links.send(gf[d, w], vy.at[d, w, rows[d]], vo.at[w, rows[d]], to_y[d])
            if w == 1:
                for h in range(2):
                    divide(number(y, 0), h, vx)
                user_work(6)
        user_work(32)
        for w in (1, 0):
            for d in range(2):
                links.arrived(gy[d, w, 1 - d], vy.at[d, w, rows[1 - d]], from_y[d])
                for h in range(2):
                    divide(number(down if d == 0 else up, w), h, vy.at[d, w])
        for w in (1, 0):
            for d in range(2):
                links.arrived(gf[d, w], vo.at[w, rows[d]], from_y[d])
                divide(number(across, w), d, vo.at[w])
        if reduce:
            vout[...] = vnew[1]
    else:
        for h in range(2):
            links.arrived(nids[h], vnew.at[1, rows[h]], before)
        vout[...] = vnew[1]
    for copy in links.started:
        copy.wait_send()


MESSAGES = 32
LOADS = 4


def exchange(which, reduce, gather, gv, own, users_in):
    side, rank = own.shape
    half = side // 2
    users = users_in is not None
    count = 8
    vmem = pl.BlockSpec(memory_space=pltpu.VMEM)
    args = ([on_chip(gv)] if reduce else []) + [on_chip(own)]
    in_specs = [vmem] * len(args)
    if users and not reduce:
        args.append(off_chip(users_in))
        in_specs.append(pl.BlockSpec(memory_space=pl.ANY))
    elif users:
        args.append(on_chip(users_in))
        in_specs.append(vmem)
    outs = []
    if reduce:
        outs.append(chip_array((side, rank), F32))
    if gather:
        outs.append(chip_array((count, 2 * side, rank), BF16))
    if users:
        blocks = users_in.shape[0]
        outs.append(chip_array((blocks, 2 * side, rank), BF16))
        outs.append(chip_array((blocks, side, rank), F32))
    scratch = []
    if reduce:
        scratch += [
            pltpu.VMEM((2, 2, half, rank), F32),
            pltpu.VMEM((2, 2, half, rank), F32),
            pltpu.VMEM((2, 2, side, rank), F32),
            pltpu.VMEM((2, side, rank), F32),
            pltpu.VMEM((2, side, rank), F32),
        ]
    if gather:
        scratch += [
            pltpu.VMEM((side, rank), F32),
            pltpu.VMEM((2, 2, side, rank), F32),
            pltpu.VMEM((2, side, rank), F32),
        ]
    if users and not reduce:
        scratch += [pltpu.VMEM((blocks, side, rank), F32), pltpu.SemaphoreType.DMA((LOADS,))]
    scratch += [pltpu.SemaphoreType.DMA((MESSAGES,))] * 2
    return pl.pallas_call(
        functools.partial(exchange_kernel, reduce, gather, users),
        out_shape=tuple(outs),
        in_specs=in_specs,
        out_specs=(vmem,) * len(outs),
        scratch_shapes=scratch,
        compiler_params=pltpu.CompilerParams(
            collective_id=which, has_side_effects=True, vmem_limit_bytes=VMEM_LIMIT
        ),
        name=f"exchange{which}",
    )(*args)


def local(user_factors, item_factors, block_index, block_count, ratings):
    side = ratings.shape[-1]
    rank = user_factors.shape[1]
    users = user_factors.reshape(-1, side, rank)
    vhl, uhl, ubase = exchange(0, False, True, None, item_factors, users)
    own = item_factors
    for step in range(STEPS):
        users, gv, *final = local_grads(step, block_index, block_count, uhl, vhl, ubase, ratings)
        if step < STEPS - 1:
            own, vhl, uhl, ubase = exchange(1, True, True, gv, own, users)
        else:
            (own,) = exchange(2, True, False, gv, own, None)
    return (final[0].reshape(user_factors.shape), own)


def solution(mesh):
    in_specs = (
        P(("blk", "user"), None),
        P(("blk", "user"), None),
        P(None, ("blk", "user"), None, None),
        P(None, ("blk", "user"), None),
        P(None, ("blk", "user"), None, None, None, None),
    )
    out_specs = (P(("blk", "user"), None), P(("blk", "user"), None))
    return jax.shard_map(local, mesh=mesh, in_specs=in_specs, out_specs=out_specs, check_vma=False)
```

```python
import functools

import jax
import jax.numpy as jnp
from jax import lax
from jax.experimental import pallas as pl
from jax.experimental.pallas import tpu as pltpu
from jax.sharding import PartitionSpec as P

STEPS = 3
USER_RATE = 0.01
ITEM_RATE = 0.0015
DECAY = 0.05
MESH = pl.DeviceIdType.MESH
F32 = jnp.float32
BF16 = jnp.bfloat16
GROUP = 4
VMEM_LIMIT = 16 << 20
COPY_IN = False


def split(x):
    hi = x.astype(BF16)
    return hi, (x - hi.astype(F32)).astype(BF16)


def chip_array(shape, dtype):
    return pltpu.VMEM(shape, dtype)


def on_chip(x):
    return pltpu.with_memory_space_constraint(x, pltpu.VMEM)


def off_chip(x):
    return pltpu.with_memory_space_constraint(x, pltpu.HBM)


def matmul(a, b, dims=((1,), (0,))):
    return lax.dot_general(a, b, (dims, ((), ())), preferred_element_type=F32)


def grads_kernel(step, idx, cnt, uhl, vhl, ubase, ratings, unew, gv, *refs):
    final, out_sems = (refs[0], refs[-1]) if step == STEPS - 1 else (None, None)
    psc, rsc, tsc = refs[1:4] if step == STEPS - 1 else refs
    rows, cols = cnt.shape[1], cnt.shape[2]
    tiles = rows * cols
    side = psc.shape[1]
    slots = idx.shape[3]
    sub = uhl.shape[0] // rows
    never = 1 << 20

    total = 0
    for t in range(rows):
        for c in range(cols):
            total = total + cnt[step, t, c]
    groups = lax.div(total + (GROUP - 1), GROUP)

    def locate(tile, slot):
        near = jnp.minimum(tile, tiles - 1)
        t, c = lax.div(near, cols), lax.rem(near, cols)
        q = idx[step, t, c, slot]
        last = slot + 1 >= cnt[step, t, c]
        spot = (t * sub + lax.div(q, sub), c * sub + lax.rem(q, sub), near * slots + slot)
        return spot, jnp.where(last, tile + 1, tile), jnp.where(last, 0, slot + 1)

    def group_at(cursor):
        spots, floors = [], []
        tile, slot = cursor
        for _ in range(GROUP):
            floors.append(jnp.where(tile < tiles, 0, never))
            spot, tile, slot = locate(tile, slot)
            spots += spot
        return (*spots, *floors), (tile, slot)

    def predict(group):
        for g in range(GROUP):
            row, item = group[3 * g], group[3 * g + 1]
            parts = matmul(uhl[row], vhl[item], ((1,), (1,)))
            psc[g] = parts[:side, :side] + (parts[:side, side:] + parts[side:, :side])

    def residual(group, over):
        for g in range(GROUP):
            rating = ratings[group[3 * g + 2]]
            floor = jnp.where(over, never, group[3 * GROUP + g])
            res = jnp.where(rating > floor, 0.5 * rating.astype(F32) - psc[g], 0.0)
            for into, x in ((rsc, res), (tsc, res.T)):
                hi, lo = split(x)
                into[g, 0] = hi
                into[g, 1] = lo

    def product(left, g, right):
        hi, lo = left[g, 0], left[g, 1]
        twice = jnp.concatenate(
            [jnp.concatenate([hi, hi], axis=1), jnp.concatenate([lo, lo], axis=1)], axis=0
        )
        both = matmul(twice, right[...])
        return both[:side] + both[side:]

    def update(group):
        for g in range(GROUP):
            row, item = group[3 * g], group[3 * g + 1]
            unew[row] += USER_RATE * product(rsc, g, vhl.at[item])
            gv[item] += product(tsc, g, uhl.at[row])

    def put(row):
        part = pl.ds(row * sub, sub)
        return pltpu.make_async_copy(unew.at[part], final.at[part], out_sems.at[row])

    def start_put(row, carry):
        put(row).start()
        return carry

    gv[...] = jnp.zeros_like(gv)
    if COPY_IN:
        unew[...] = ubase[...]
    one, cursor = group_at((jnp.int32(0), jnp.int32(0)))
    predict(one)
    residual(one, False)
    two, cursor = group_at(cursor)
    predict(two)

    def body(i, carry):
        now, coming, cursor = carry
        fresh, cursor = group_at(cursor)
        update(now)
        residual(coming, i + 1 >= groups)
        predict(fresh)
        if final is not None:
            here, there = (lax.div(group[2], cols * slots) for group in (now, coming))
            lax.fori_loop(here, jnp.where(i + 1 >= groups, rows, there), start_put, 0)
        return coming, fresh, cursor

    lax.fori_loop(0, groups, body, (one, two, cursor))
    if final is not None:
        for row in range(rows):
            put(row).wait()


def local_grads(step, idx, cnt, uhl, vhl, ubase, ratings):
    side = ratings.shape[-1]
    rank = ubase.shape[-1]
    vmem = pl.BlockSpec(memory_space=pltpu.VMEM)
    smem = pl.BlockSpec(memory_space=pltpu.SMEM)
    outs = [chip_array(ubase.shape, F32), chip_array((vhl.shape[0], side, rank), F32)]
    out_specs = [vmem, vmem]
    scratch = [pltpu.VMEM((GROUP, side, side), F32)] + [pltpu.VMEM((GROUP, 2, side, side), BF16)] * 2
    if step == STEPS - 1:
        outs.append(jax.ShapeDtypeStruct(ubase.shape, F32))
        out_specs.append(pl.BlockSpec(memory_space=pl.ANY))
        scratch.append(pltpu.SemaphoreType.DMA((cnt.shape[1],)))
    return pl.pallas_call(
        functools.partial(grads_kernel, step),
        out_shape=tuple(outs),
        in_specs=[smem, smem, vmem, vmem, vmem, vmem],
        out_specs=tuple(out_specs),
        scratch_shapes=scratch,
        input_output_aliases={4: 0},
        compiler_params=pltpu.CompilerParams(vmem_limit_bytes=VMEM_LIMIT),
        name=f"grads{step}",
    )(idx, cnt, on_chip(uhl), on_chip(vhl), on_chip(ubase), on_chip(ratings))


class Links:
    def __init__(self, sends, recvs):
        self.sends, self.recvs = sends, recvs
        self.started = []
        self.count = 0

    def message(self):
        self.count += 1
        return self.count - 1

    def copy(self, number, src, dst, device):
        return pltpu.make_async_remote_copy(
            src_ref=src,
            dst_ref=dst,
            send_sem=self.sends.at[number],
            recv_sem=self.recvs.at[number],
            device_id=device,
            device_id_type=MESH,
        )

    def send(self, number, src, dst, device):
        copy = self.copy(number, src, dst, device)
        copy.start()
        self.started.append(copy)

    def arrived(self, number, dst, device):
        self.copy(number, dst, dst, device).wait_recv()


PARTS = ((0, 48), (48, 48), (96, 32))


def part_halves(part):
    first, size = part
    return (pl.ds(first, size // 2), pl.ds(first + size // 2, size // 2))


def exchange_kernel(step, reduce, gather, *refs):
    refs = list(refs)
    gv = refs.pop(0) if reduce else None
    vin = refs.pop(0)
    uin, rin_hbm = (refs.pop(0), refs.pop(0)) if gather else (None, None)
    vout = refs.pop(0) if reduce else None
    vhl, uhl, ubase, rout = (refs.pop(0) for _ in range(4)) if gather else (None,) * 4
    if reduce:
        xin, xsum, opp, stage, rin, xio, vnew = (refs.pop(0) for _ in range(7))
    if gather:
        vx, vy, vo = (refs.pop(0) for _ in range(3))
    if gather and not reduce:
        uraw = refs.pop(0)
    if gather:
        load_sems, rate_sem = refs.pop(0), refs.pop(0)
    sends, recvs = refs

    loads = []
    if gather:
        if not reduce:
            span = uin.shape[0] // LOADS
            for i in range(LOADS):
                piece = pl.ds(i * span, span)
                loads.append(pltpu.make_async_copy(uin.at[piece], uraw.at[piece], load_sems.at[i]))
            for load in loads:
                load.start()
            uin = uraw
        rates = pltpu.make_async_copy(rin_hbm.at[step], rout, rate_sem)
        rates.start()

    blk, user = lax.axis_index("blk"), lax.axis_index("user")
    blks = lax.axis_size("blk")
    y, xl = lax.div(user, 2), lax.rem(user, 2)
    ys = lax.axis_size("user") // 2
    up, down, across = lax.rem(y + 1, ys), lax.rem(y + ys - 1, ys), lax.rem(y + 2, ys)
    near = (up, down)
    to_y = ((blk, up * 2 + xl), (blk, down * 2 + xl))
    from_y = (to_y[1], to_y[0])
    to_x = (blk, y * 2 + 1 - xl)
    after = (lax.rem(blk + 1, blks), user)
    before = (lax.rem(blk + blks - 1, blks), user)

    def number(row, which):
        return row * 2 + (1 - xl if which == 0 else xl)

    side = vin.shape[0]
    halves = [part_halves(part) for part in PARTS]
    whole = [pl.ds(*part) for part in PARTS]
    links = Links(sends, recvs)
    both = (0, 1)

    done = [0]

    def user_work(amount):
        if not gather:
            return
        blocks = uin.shape[0]
        start = done[0]
        stop = min(blocks, start + amount)
        done[0] = stop
        if start == stop:
            return
        while loads and (LOADS - len(loads)) * (blocks // LOADS) < stop:
            loads.pop(0).wait()

        def one(i, carry):
            x = uin[i]
            hi, lo = split(x)
            uhl[i, :side] = hi
            uhl[i, side:] = lo
            ubase[i] = x * (1.0 - USER_RATE * DECAY)
            return carry

        lax.fori_loop(start, stop, one, 0)

    barrier = pltpu.get_barrier_semaphore()
    greet = [to_y[0], to_y[1], to_x] + ([before] if reduce else [])
    for device in greet:
        pl.semaphore_signal(barrier, inc=1, device_id=device, device_id_type=MESH)
    pl.semaphore_wait(barrier, len(greet))

    ids = {}

    def number_of(*key):
        if key not in ids:
            ids[key] = links.message()
        return ids[key]

    def send(key, src, dst, device):
        links.send(number_of(*key), src, dst, device)

    def arrived(key, dst, device):
        links.arrived(number_of(*key), dst, device)


    def first_sends(p):
        for w in both:
            for d in both:
                send(("A", p, d, w), gv.at[number(across, w), halves[p][d]], opp.at[d, w, halves[p][d]], to_y[d])
        for w in both:
            for d in both:
                rows = halves[p][1 - d]
                send(("B", p, d, w), gv.at[number(near[d], w), rows], rin.at[d, w, rows], to_y[d])

    def second_sends(p):
        for w in both:
            for d in both:
                rows = halves[p][d]
                arrived(("A", p, d, w), opp.at[d, w, rows], from_y[d])
                stage[d, w, rows] = gv[number(near[d], w), rows] + opp[d, w, rows]
                send(("C", p, d, w), stage.at[d, w, rows], rin.at[d, w, rows], to_y[d])

    def received(p, w):
        for d in both:
            arrived(("B", p, d, w), rin.at[d, w, halves[p][1 - d]], from_y[d])
            arrived(("C", p, d, w), rin.at[d, w, halves[p][d]], from_y[d])

    def to_partner(p):
        rows = whole[p]
        received(p, 0)
        xio[0, rows] = gv[number(y, 0), rows] + (rin[0, 0, rows] + rin[1, 0, rows])
        send(("X", p), xio.at[0, rows], xio.at[1, rows], to_x)

    def renew(p, own):
        rows = whole[p]
        received(p, 1)
        grad = own() + (rin[0, 1, rows] + rin[1, 1, rows])
        old = vin[rows]
        vnew[0, rows] = old + ITEM_RATE * (grad - DECAY * old)
        send(("N", p), vnew.at[0, rows], vnew.at[1, rows], after)

    def own_sum(p):
        rows = whole[p]
        arrived(("X", p), xio.at[1, rows], to_x)
        return gv[number(y, 1), rows] + xio[1, rows]


    if gather:
        own = vnew.at[1] if reduce else vin

        def open_part(p):
            rows = whole[p]
            if reduce:
                arrived(("N", p), vnew.at[1, rows], before)
            for d in both:
                send(("GY", p, d, 1), own.at[rows], vy.at[d, 1, rows], to_y[d])
            send(("GX", p, 0), own.at[rows], vx.at[rows], to_x)

        def pass_partner(p):
            rows = whole[p]
            arrived(("GX", p, 0), vx.at[rows], to_x)
            for d in both:
                send(("GY", p, d, 0), vx.at[rows], vy.at[d, 0, rows], to_y[d])

        def pass_on(p, w):
            for d in both:
                arrived(("GY", p, d, w), vy.at[d, w, whole[p]], from_y[d])
                rows = halves[p][d]
                send(("GF", p, d, w), vy.at[d, w, rows], vo.at[w, rows], to_y[d])

        def pass_x(p):
            for d in both:
                send(("GX", p, 1 + d), vy.at[d, 1, whole[p]], vy.at[d, 0, whole[p]], to_x)

        def last(p, w):
            for d in both:
                arrived(("GF", p, d, w), vo.at[w, halves[p][d]], from_y[d])

        def divide(block, ref):
            hi, lo = split(ref[...])
            vhl[block, :side] = hi
            vhl[block, side:] = lo

    if reduce:
        x = 0
        roles = (across, up, down, y)
        for r in range(4):
            send(("S", r), gv.at[number(roles[r], 0), whole[x]], xin.at[r], to_x)
        first_sends(1)

        size = PARTS[x][1]
        cut = (pl.ds(0, size // 2), pl.ds(size // 2, size // 2))

        def with_partner(r):
            arrived(("S", r), xin.at[r], to_x)
            xsum[r] = gv[number(roles[r], 1), whole[x]] + xin[r]

        user_work(4)
        with_partner(0)
        for d in both:
            send(("A", x, d, 1), xsum.at[0, cut[d]], opp.at[d, 1, halves[x][d]], to_y[d])
        for d in both:
            with_partner(1 + d)
            rows = halves[x][1 - d]
            send(("B", x, d, 1), xsum.at[1 + d, cut[1 - d]], rin.at[d, 1, rows], to_y[d])
        second_sends(1)
        first_sends(2)
        for d in both:
            rows = halves[x][d]
            arrived(("A", x, d, 1), opp.at[d, 1, rows], from_y[d])
            stage[d, 1, rows] = xsum[1 + d, cut[d]] + opp[d, 1, rows]
            send(("C", x, d, 1), stage.at[d, 1, rows], rin.at[d, 1, rows], to_y[d])
        with_partner(3)
        user_work(3)
        to_partner(1)
        second_sends(2)
        renew(x, lambda: xsum[3])
        user_work(3)
        renew(1, lambda: own_sum(1))
        to_partner(2)
        if gather:
            open_part(0)
            open_part(1)
        renew(2, lambda: own_sum(2))
    elif gather:
        for p in range(3):
            open_part(p)
        user_work(2)

    if gather:
        user_work(2)
        pass_on(0, 1)
        pass_x(0)
        pass_partner(1)
        if reduce:
            open_part(2)
        pass_on(1, 1)
        user_work(2)
        last(0, 1)
        send(("GX", 0, 3), vo.at[1, whole[0]], vo.at[0, whole[0]], to_x)
        pass_partner(2)
        user_work(2)
        pass_on(1, 0)
        user_work(2)
        pass_on(2, 1)
        user_work(2)
        pass_on(2, 0)
        user_work(32)
        divide(user, own)
        arrived(("GX", 0, 0), vx.at[whole[0]], to_x)
        divide(number(y, 0), vx)
        for d in both:
            divide(number((down, up)[d], 1), vy.at[d, 1])
            arrived(("GX", 0, 1 + d), vy.at[d, 0, whole[0]], to_x)
            divide(number((down, up)[d], 0), vy.at[d, 0])
        if reduce:
            vout[...] = vnew[1]
        arrived(("GX", 0, 3), vo.at[0, whole[0]], to_x)
        for w in (1, 0):
            for p in (1, 2):
                last(p, w)
            divide(number(across, w), vo.at[w])
        rates.wait()
    else:
        for p in range(3):
            arrived(("N", p), vnew.at[1, whole[p]], before)
        vout[...] = vnew[1]
    for copy in links.started:
        copy.wait_send()


MESSAGES = 72
LOADS = 4


def exchange(which, step, gv, own, users_in, ratings):
    reduce, gather = gv is not None, users_in is not None
    side, rank = own.shape
    size = PARTS[0][1]
    vmem = pl.BlockSpec(memory_space=pltpu.VMEM)
    anywhere = pl.BlockSpec(memory_space=pl.ANY)
    args = ([on_chip(gv)] if reduce else []) + [on_chip(own)]
    in_specs = [vmem] * len(args)
    outs, scratch = [], []
    if reduce:
        outs.append(chip_array((side, rank), F32))
        scratch += [
            pltpu.VMEM((4, size, rank), F32),
            pltpu.VMEM((4, size, rank), F32),
            pltpu.VMEM((2, 2, side, rank), F32),
            pltpu.VMEM((2, 2, side, rank), F32),
            pltpu.VMEM((2, 2, side, rank), F32),
            pltpu.VMEM((2, side, rank), F32),
            pltpu.VMEM((2, side, rank), F32),
        ]
    if gather:
        blocks = users_in.shape[0]
        args += [on_chip(users_in) if reduce else off_chip(users_in), off_chip(ratings)]
        in_specs += [vmem if reduce else anywhere, anywhere]
        outs += [
            chip_array((8, 2 * side, rank), BF16),
            chip_array((blocks, 2 * side, rank), BF16),
            chip_array((blocks, side, rank), F32),
            chip_array(ratings.shape[1:], jnp.int32),
        ]
        scratch += [
            pltpu.VMEM((side, rank), F32),
            pltpu.VMEM((2, 2, side, rank), F32),
            pltpu.VMEM((2, side, rank), F32),
        ]
        if not reduce:
            scratch.append(pltpu.VMEM((blocks, side, rank), F32))
        scratch += [pltpu.SemaphoreType.DMA((LOADS,)), pltpu.SemaphoreType.DMA]
    scratch += [pltpu.SemaphoreType.DMA((MESSAGES,))] * 2
    return pl.pallas_call(
        functools.partial(exchange_kernel, step, reduce, gather),
        out_shape=tuple(outs),
        in_specs=in_specs,
        out_specs=(vmem,) * len(outs),
        scratch_shapes=scratch,
        compiler_params=pltpu.CompilerParams(
            collective_id=which, has_side_effects=True, vmem_limit_bytes=VMEM_LIMIT
        ),
        name=f"exchange{which}",
    )(*args)


def local(user_factors, item_factors, block_index, block_count, ratings):
    side = ratings.shape[-1]
    rank = user_factors.shape[1]
    users = user_factors.reshape(-1, side, rank)
    flat = ratings.reshape(STEPS, -1, side, side)
    vhl, uhl, ubase, rates = exchange(0, 0, None, item_factors, users, flat)
    own = item_factors
    for step in range(STEPS):
        users, gv, *final = local_grads(step, block_index, block_count, uhl, vhl, ubase, rates)
        if step < STEPS - 1:
            own, vhl, uhl, ubase, rates = exchange(step + 1, step + 1, gv, own, users, flat)
        else:
            (own,) = exchange(STEPS, 0, gv, own, None, None)
    return (final[0].reshape(user_factors.shape), own)


def solution(mesh):
    in_specs = (
        P(("blk", "user"), None),
        P(("blk", "user"), None),
        P(None, ("blk", "user"), None, None),
        P(None, ("blk", "user"), None),
        P(None, ("blk", "user"), None, None, None, None),
    )
    out_specs = (P(("blk", "user"), None), P(("blk", "user"), None))
    return jax.shard_map(local, mesh=mesh, in_specs=in_specs, out_specs=out_specs, check_vma=False)
```

```python
import functools

import jax
import jax.numpy as jnp
from jax import lax
from jax.experimental import pallas as pl
from jax.experimental.pallas import tpu as pltpu
from jax.sharding import PartitionSpec as P

STEPS = 3
USER_RATE = 0.01
ITEM_RATE = 0.0015
DECAY = 0.05
MESH = pl.DeviceIdType.MESH
F32 = jnp.float32
BF16 = jnp.bfloat16
GROUP = 4
VMEM_LIMIT = 16 << 20
COPY_IN = False


def split(x):
    hi = x.astype(BF16)
    return hi, (x - hi.astype(F32)).astype(BF16)


def chip_array(shape, dtype):
    return pltpu.VMEM(shape, dtype)


def on_chip(x):
    return pltpu.with_memory_space_constraint(x, pltpu.VMEM)


def off_chip(x):
    return pltpu.with_memory_space_constraint(x, pltpu.HBM)


def matmul(a, b, dims=((1,), (0,))):
    return lax.dot_general(a, b, (dims, ((), ())), preferred_element_type=F32)


def grads_kernel(step, idx, cnt, uhl, vhl, ubase, ratings, unew, gv, *refs):
    final, out_sems = (refs[0], refs[-1]) if step == STEPS - 1 else (None, None)
    psc, rsc, tsc = refs[1:4] if step == STEPS - 1 else refs
    rows, cols = cnt.shape[1], cnt.shape[2]
    tiles = rows * cols
    side = psc.shape[1]
    slots = idx.shape[3]
    sub = uhl.shape[0] // rows
    never = 1 << 20

    total = 0
    for t in range(rows):
        for c in range(cols):
            total = total + cnt[step, t, c]
    groups = lax.div(total + (GROUP - 1), GROUP)

    def locate(tile, slot):
        near = jnp.minimum(tile, tiles - 1)
        t, c = lax.div(near, cols), lax.rem(near, cols)
        q = idx[step, t, c, slot]
        last = slot + 1 >= cnt[step, t, c]
        spot = (t * sub + lax.div(q, sub), c * sub + lax.rem(q, sub), near * slots + slot)
        return spot, jnp.where(last, tile + 1, tile), jnp.where(last, 0, slot + 1)

    def group_at(cursor):
        spots, floors = [], []
        tile, slot = cursor
        for _ in range(GROUP):
            floors.append(jnp.where(tile < tiles, 0, never))
            spot, tile, slot = locate(tile, slot)
            spots += spot
        return (*spots, *floors), (tile, slot)

    def predict(group):
        for g in range(GROUP):
            row, item = group[3 * g], group[3 * g + 1]
            parts = matmul(uhl[row], vhl[item], ((1,), (1,)))
            psc[g] = parts[:side, :side] + (parts[:side, side:] + parts[side:, :side])

    def residual(group, over):
        for g in range(GROUP):
            rating = ratings[group[3 * g + 2]]
            floor = jnp.where(over, never, group[3 * GROUP + g])
            res = jnp.where(rating > floor, 0.5 * rating.astype(F32) - psc[g], 0.0)
            for into, x in ((rsc, res), (tsc, res.T)):
                hi, lo = split(x)
                into[g, 0] = hi
                into[g, 1] = lo

    def product(left, g, right):
        hi, lo = left[g, 0], left[g, 1]
        twice = jnp.concatenate(
            [jnp.concatenate([hi, hi], axis=1), jnp.concatenate([lo, lo], axis=1)], axis=0
        )
        both = matmul(twice, right[...])
        return both[:side] + both[side:]

    def update(group):
        for g in range(GROUP):
            row, item = group[3 * g], group[3 * g + 1]
            unew[row] += USER_RATE * product(rsc, g, vhl.at[item])
            gv[item] += product(tsc, g, uhl.at[row])

    def put(row):
        part = pl.ds(row * sub, sub)
        return pltpu.make_async_copy(unew.at[part], final.at[part], out_sems.at[row])

    def start_put(row, carry):
        put(row).start()
        return carry

    gv[...] = jnp.zeros_like(gv)
    if COPY_IN:
        unew[...] = ubase[...]
    one, cursor = group_at((jnp.int32(0), jnp.int32(0)))
    predict(one)
    residual(one, False)
    two, cursor = group_at(cursor)
    predict(two)

    def body(i, carry):
        now, coming, cursor = carry
        fresh, cursor = group_at(cursor)
        update(now)
        residual(coming, i + 1 >= groups)
        predict(fresh)
        if final is not None:
            here, there = (lax.div(group[2], cols * slots) for group in (now, coming))
            lax.fori_loop(here, jnp.where(i + 1 >= groups, rows, there), start_put, 0)
        return coming, fresh, cursor

    lax.fori_loop(0, groups, body, (one, two, cursor))
    if final is not None:
        for row in range(rows):
            put(row).wait()


def local_grads(step, idx, cnt, uhl, vhl, ubase, ratings):
    side = ratings.shape[-1]
    rank = ubase.shape[-1]
    vmem = pl.BlockSpec(memory_space=pltpu.VMEM)
    smem = pl.BlockSpec(memory_space=pltpu.SMEM)
    outs = [chip_array(ubase.shape, F32), chip_array((vhl.shape[0], side, rank), F32)]
    out_specs = [vmem, vmem]
    scratch = [pltpu.VMEM((GROUP, side, side), F32)] + [pltpu.VMEM((GROUP, 2, side, side), BF16)] * 2
    if step == STEPS - 1:
        outs.append(jax.ShapeDtypeStruct(ubase.shape, F32))
        out_specs.append(pl.BlockSpec(memory_space=pl.ANY))
        scratch.append(pltpu.SemaphoreType.DMA((cnt.shape[1],)))
    return pl.pallas_call(
        functools.partial(grads_kernel, step),
        out_shape=tuple(outs),
        in_specs=[smem, smem, vmem, vmem, vmem, vmem],
        out_specs=tuple(out_specs),
        scratch_shapes=scratch,
        input_output_aliases={4: 0},
        compiler_params=pltpu.CompilerParams(vmem_limit_bytes=VMEM_LIMIT),
        name=f"grads{step}",
    )(idx, cnt, on_chip(uhl), on_chip(vhl), on_chip(ubase), on_chip(ratings))


class Links:
    def __init__(self, sends, recvs):
        self.sends, self.recvs = sends, recvs
        self.started = []
        self.count = 0

    def message(self):
        self.count += 1
        return self.count - 1

    def copy(self, number, src, dst, device):
        return pltpu.make_async_remote_copy(
            src_ref=src,
            dst_ref=dst,
            send_sem=self.sends.at[number],
            recv_sem=self.recvs.at[number],
            device_id=device,
            device_id_type=MESH,
        )

    def send(self, number, src, dst, device):
        copy = self.copy(number, src, dst, device)
        copy.start()
        self.started.append(copy)

    def arrived(self, number, dst, device):
        self.copy(number, dst, dst, device).wait_recv()


def exchange_kernel(step, reduce, gather, *refs):
    users = gather
    refs = list(refs)
    gv = refs.pop(0) if reduce else None
    vin = refs.pop(0)
    uin, rates_in = (refs.pop(0), refs.pop(0)) if gather else (None, None)
    vout = refs.pop(0) if reduce else None
    vhl, uhl, ubase, rates_out = (refs.pop(0) for _ in range(4)) if gather else (None,) * 4
    if reduce:
        opp, stage, rin, xio, vnew = (refs.pop(0) for _ in range(5))
    if gather:
        vx, vy, vo = (refs.pop(0) for _ in range(3))
    uraw = refs.pop(0) if gather and not reduce else None
    load_sems, rate_sem = (refs.pop(0), refs.pop(0)) if gather else (None, None)
    sends, recvs = refs

    blk, user = lax.axis_index("blk"), lax.axis_index("user")
    blks = lax.axis_size("blk")
    y, xl = lax.div(user, 2), lax.rem(user, 2)
    ys = lax.axis_size("user") // 2
    up, down, across = lax.rem(y + 1, ys), lax.rem(y + ys - 1, ys), lax.rem(y + 2, ys)
    to_y = ((blk, up * 2 + xl), (blk, down * 2 + xl))
    from_y = (to_y[1], to_y[0])
    to_x = (blk, y * 2 + 1 - xl)
    after = (lax.rem(blk + 1, blks), user)
    before = (lax.rem(blk + blks - 1, blks), user)

    def number(row, which):
        return row * 2 + (1 - xl if which == 0 else xl)

    side = vin.shape[0]
    half = side // 2
    rows = (pl.ds(0, half), pl.ds(half, half))
    links = Links(sends, recvs)

    loads = []
    rates = []

    def start_loads():
        if gather:
            if not reduce:
                span = uin.shape[0] // LOADS
                for i in range(LOADS):
                    piece = pl.ds(i * span, span)
                    loads.append(pltpu.make_async_copy(uin.at[piece], uraw.at[piece], load_sems.at[i]))
                for load in loads:
                    load.start()
            rates.append(pltpu.make_async_copy(rates_in.at[step], rates_out, rate_sem))
            rates[0].start()

    uwork = uraw if uraw is not None else uin
    todo = [0]
    if users:
        blocks = uin.shape[0]

        def user_work(amount):
            start = todo[0]
            stop = min(blocks, start + amount)
            todo[0] = stop
            if start == stop:
                return
            while loads and (LOADS - len(loads)) * (blocks // LOADS) < stop:
                loads.pop(0).wait()

            def one(i, carry):
                x = uwork[i]
                hi, lo = split(x)
                uhl[i, :side] = hi
                uhl[i, side:] = lo
                ubase[i] = x * (1.0 - USER_RATE * DECAY)
                return carry

            lax.fori_loop(start, stop, one, 0)
    else:

        def user_work(amount):
            pass

    barrier = pltpu.get_barrier_semaphore()
    greet = [to_y[0], to_y[1], to_x] + ([before] if reduce else [])
    for device in greet:
        pl.semaphore_signal(barrier, inc=1, device_id=device, device_id_type=MESH)
    pl.semaphore_wait(barrier, len(greet))

    if reduce:
        ids = {}
        for kind in "ABC":
            for d in range(2):
                for w in range(2):
                    ids[kind, d, w] = links.message()
        for w in range(2):
            for d in range(2):
                links.send(ids["A", d, w], gv.at[number(across, w), rows[d]], opp.at[d, w], to_y[d])
            for d in range(2):
                near = up if d == 0 else down
                links.send(
                    ids["B", d, w], gv.at[number(near, w), rows[1 - d]], rin.at[d, w, rows[1 - d]], to_y[d]
                )
        start_loads()
        user_work(6)
        xids = [links.message() for _ in range(2)]
        for w in range(2):
            for d in range(2):
                near = up if d == 0 else down
                links.arrived(ids["A", d, w], opp.at[d, w], from_y[d])
                stage[d, w] = gv[number(near, w), rows[d]] + opp[d, w]
                links.send(ids["C", d, w], stage.at[d, w], rin.at[d, w, rows[d]], to_y[d])
            if w == 0:
                user_work(4)
        for h in range(2):
            links.arrived(ids["B", 1 - h, 0], rin.at[1 - h, 0, rows[h]], from_y[1 - h])
            links.arrived(ids["C", h, 0], rin.at[h, 0, rows[h]], from_y[h])
            xio[0, rows[h]] = gv[number(y, 0), rows[h]] + (rin[0, 0, rows[h]] + rin[1, 0, rows[h]])
            links.send(xids[h], xio.at[0, rows[h]], xio.at[1, rows[h]], to_x)
        user_work(8)
        nids = [links.message() for _ in range(2)]
        for h in range(2):
            links.arrived(ids["B", 1 - h, 1], rin.at[1 - h, 1, rows[h]], from_y[1 - h])
            links.arrived(ids["C", h, 1], rin.at[h, 1, rows[h]], from_y[h])
            links.arrived(xids[h], xio.at[1, rows[h]], to_x)
            grad = (gv[number(y, 1), rows[h]] + (rin[0, 1, rows[h]] + rin[1, 1, rows[h]])) + xio[1, rows[h]]
            old = vin[rows[h]]
            vnew[0, rows[h]] = old + ITEM_RATE * (grad - DECAY * old)
            links.send(nids[h], vnew.at[0, rows[h]], vnew.at[1, rows[h]], after)

    if gather:
        own = vnew.at[1] if reduce else vin
        gx = [links.message() for _ in range(2)]
        gy = {(d, w, h): links.message() for d in range(2) for w in range(2) for h in range(2)}
        gf = {(d, w): links.message() for d in range(2) for w in range(2)}

        def divide(block, h, ref):
            hi, lo = split(ref[rows[h]])
            vhl[block, rows[h]] = hi
            vhl[block, pl.ds(side + h * half, half)] = lo

        for h in range(2):
            if reduce:
                links.arrived(nids[h], vnew.at[1, rows[h]], before)
            links.send(gx[h], own.at[rows[h]], vx.at[rows[h]], to_x)
            for d in (h, 1 - h):
                links.send(gy[d, 1, h], own.at[rows[h]], vy.at[d, 1, rows[h]], to_y[d])
        if not reduce:
            start_loads()
        for h in range(2):
            divide(user, h, own)
        if reduce:
            user_work(4)
        for h in range(2):
            links.arrived(gx[h], vx.at[rows[h]], to_x)
            for d in (h, 1 - h):
                links.send(gy[d, 0, h], vx.at[rows[h]], vy.at[d, 0, rows[h]], to_y[d])
        for w in (1, 0):
            for d in range(2):
                links.arrived(gy[d, w, d], vy.at[d, w, rows[d]], from_y[d])
                links.send(gf[d, w], vy.at[d, w, rows[d]], vo.at[w, rows[d]], to_y[d])
            if w == 1:
                for h in range(2):
                    divide(number(y, 0), h, vx)
                user_work(6)
        user_work(32)
        for w in (1, 0):
            for d in range(2):
                links.arrived(gy[d, w, 1 - d], vy.at[d, w, rows[1 - d]], from_y[d])
                for h in range(2):
                    divide(number(down if d == 0 else up, w), h, vy.at[d, w])
        for w in (1, 0):
            for d in range(2):
                links.arrived(gf[d, w], vo.at[w, rows[d]], from_y[d])
                divide(number(across, w), d, vo.at[w])
        if reduce:
            vout[...] = vnew[1]
        rates[0].wait()
    else:
        for h in range(2):
            links.arrived(nids[h], vnew.at[1, rows[h]], before)
        vout[...] = vnew[1]
    for copy in links.started:
        copy.wait_send()


MESSAGES = 32
LOADS = 4


def exchange(which, step, gv, own, users_in, ratings):
    reduce, gather = gv is not None, users_in is not None
    side, rank = own.shape
    half = side // 2
    vmem = pl.BlockSpec(memory_space=pltpu.VMEM)
    anywhere = pl.BlockSpec(memory_space=pl.ANY)
    args = ([on_chip(gv)] if reduce else []) + [on_chip(own)]
    in_specs = [vmem] * len(args)
    outs, scratch = [], []
    if reduce:
        outs.append(chip_array((side, rank), F32))
        scratch += [
            pltpu.VMEM((2, 2, half, rank), F32),
            pltpu.VMEM((2, 2, half, rank), F32),
            pltpu.VMEM((2, 2, side, rank), F32),
            pltpu.VMEM((2, side, rank), F32),
            pltpu.VMEM((2, side, rank), F32),
        ]
    if gather:
        blocks = users_in.shape[0]
        args += [on_chip(users_in) if reduce else off_chip(users_in), off_chip(ratings)]
        in_specs += [vmem if reduce else anywhere, anywhere]
        outs += [
            chip_array((8, 2 * side, rank), BF16),
            chip_array((blocks, 2 * side, rank), BF16),
            chip_array((blocks, side, rank), F32),
            chip_array(ratings.shape[1:], jnp.int32),
        ]
        scratch += [
            pltpu.VMEM((side, rank), F32),
            pltpu.VMEM((2, 2, side, rank), F32),
            pltpu.VMEM((2, side, rank), F32),
        ]
        if not reduce:
            scratch.append(pltpu.VMEM((blocks, side, rank), F32))
        scratch += [pltpu.SemaphoreType.DMA((LOADS,)), pltpu.SemaphoreType.DMA]
    scratch += [pltpu.SemaphoreType.DMA((MESSAGES,))] * 2
    return pl.pallas_call(
        functools.partial(exchange_kernel, step, reduce, gather),
        out_shape=tuple(outs),
        in_specs=in_specs,
        out_specs=(vmem,) * len(outs),
        scratch_shapes=scratch,
        compiler_params=pltpu.CompilerParams(
            collective_id=which, has_side_effects=True, vmem_limit_bytes=VMEM_LIMIT
        ),
        name=f"exchange{which}",
    )(*args)


def local(user_factors, item_factors, block_index, block_count, ratings):
    side = ratings.shape[-1]
    rank = user_factors.shape[1]
    users = user_factors.reshape(-1, side, rank)
    flat = ratings.reshape(STEPS, -1, side, side)
    vhl, uhl, ubase, rates = exchange(0, 0, None, item_factors, users, flat)
    own = item_factors
    for step in range(STEPS):
        users, gv, *final = local_grads(step, block_index, block_count, uhl, vhl, ubase, rates)
        if step < STEPS - 1:
            own, vhl, uhl, ubase, rates = exchange(step + 1, step + 1, gv, own, users, flat)
        else:
            (own,) = exchange(STEPS, 0, gv, own, None, None)
    return (final[0].reshape(user_factors.shape), own)


def solution(mesh):
    in_specs = (
        P(("blk", "user"), None),
        P(("blk", "user"), None),
        P(None, ("blk", "user"), None, None),
        P(None, ("blk", "user"), None),
        P(None, ("blk", "user"), None, None, None, None),
    )
    out_specs = (P(("blk", "user"), None), P(("blk", "user"), None))
    return jax.shard_map(local, mesh=mesh, in_specs=in_specs, out_specs=out_specs, check_vma=False)
```

```python
import functools

import jax
import jax.numpy as jnp
from jax import lax
from jax.experimental import pallas as pl
from jax.experimental.pallas import tpu as pltpu
from jax.sharding import PartitionSpec as P

STEPS = 3
USER_RATE = 0.01
ITEM_RATE = 0.0015
DECAY = 0.05
MESH = pl.DeviceIdType.MESH
F32 = jnp.float32
BF16 = jnp.bfloat16
GROUP = 4
VMEM_LIMIT = 16 << 20
COPY_IN = False


def split(x):
    hi = x.astype(BF16)
    return hi, (x - hi.astype(F32)).astype(BF16)


def chip_array(shape, dtype):
    return pltpu.VMEM(shape, dtype)


def on_chip(x):
    return pltpu.with_memory_space_constraint(x, pltpu.VMEM)


def off_chip(x):
    return pltpu.with_memory_space_constraint(x, pltpu.HBM)


def matmul(a, b, dims=((1,), (0,))):
    return lax.dot_general(a, b, (dims, ((), ())), preferred_element_type=F32)


def grads_kernel(step, idx, cnt, uhl, vhl, ubase, ratings, unew, gv, *refs):
    final, out_sems = (refs[0], refs[-1]) if step == STEPS - 1 else (None, None)
    psc, rsc, tsc = refs[1:4] if step == STEPS - 1 else refs
    cols, rows = cnt.shape[1], cnt.shape[2]
    tiles = rows * cols
    side = psc.shape[1]
    slots = idx.shape[2]
    sub = uhl.shape[0] // rows
    never = 1 << 20

    total = 0
    for t in range(rows):
        for c in range(cols):
            total = total + cnt[step, c, t]
    groups = lax.div(total + (GROUP - 1), GROUP)

    def locate(tile, slot):
        near = jnp.minimum(tile, tiles - 1)
        t, c = lax.div(near, cols), lax.rem(near, cols)
        q = idx[step, c, slot, t]
        last = slot + 1 >= cnt[step, c, t]
        spot = (t * sub + lax.div(q, sub), c * sub + lax.rem(q, sub), near * slots + slot)
        return spot, jnp.where(last, tile + 1, tile), jnp.where(last, 0, slot + 1)

    def group_at(cursor):
        spots, floors = [], []
        tile, slot = cursor
        for _ in range(GROUP):
            floors.append(jnp.where(tile < tiles, 0, never))
            spot, tile, slot = locate(tile, slot)
            spots += spot
        return (*spots, *floors), (tile, slot)

    def predict(group):
        for g in range(GROUP):
            row, item = group[3 * g], group[3 * g + 1]
            parts = matmul(uhl[row], vhl[item], ((1,), (1,)))
            psc[g] = parts[:side, :side] + (parts[:side, side:] + parts[side:, :side])

    def residual(group, over):
        for g in range(GROUP):
            rating = ratings[group[3 * g + 2]]
            floor = jnp.where(over, never, group[3 * GROUP + g])
            res = jnp.where(rating > floor, 0.5 * rating.astype(F32) - psc[g], 0.0)
            for into, x in ((rsc, res), (tsc, res.T)):
                hi, lo = split(x)
                into[g, 0] = hi
                into[g, 1] = lo

    def product(left, g, right):
        hi, lo = left[g, 0], left[g, 1]
        twice = jnp.concatenate(
            [jnp.concatenate([hi, hi], axis=1), jnp.concatenate([lo, lo], axis=1)], axis=0
        )
        both = matmul(twice, right[...])
        return both[:side] + both[side:]

    def update(group):
        for g in range(GROUP):
            row, item = group[3 * g], group[3 * g + 1]
            unew[row] += USER_RATE * product(rsc, g, vhl.at[item])
            gv[item] += product(tsc, g, uhl.at[row])

    def put(row):
        part = pl.ds(row * sub, sub)
        return pltpu.make_async_copy(unew.at[part], final.at[part], out_sems.at[row])

    def start_put(row, carry):
        put(row).start()
        return carry

    gv[...] = jnp.zeros_like(gv)
    if COPY_IN:
        unew[...] = ubase[...]
    one, cursor = group_at((jnp.int32(0), jnp.int32(0)))
    predict(one)
    residual(one, False)
    two, cursor = group_at(cursor)
    predict(two)

    def body(i, carry):
        now, coming, cursor = carry
        fresh, cursor = group_at(cursor)
        update(now)
        residual(coming, i + 1 >= groups)
        predict(fresh)
        if final is not None:
            here, there = (lax.div(group[2], cols * slots) for group in (now, coming))
            lax.fori_loop(here, jnp.where(i + 1 >= groups, rows, there), start_put, 0)
        return coming, fresh, cursor

    lax.fori_loop(0, groups, body, (one, two, cursor))
    if final is not None:
        for row in range(rows):
            put(row).wait()


def local_grads(step, idx, cnt, uhl, vhl, ubase, ratings):
    side = ratings.shape[-1]
    rank = ubase.shape[-1]
    vmem = pl.BlockSpec(memory_space=pltpu.VMEM)
    smem = pl.BlockSpec(memory_space=pltpu.SMEM)
    outs = [chip_array(ubase.shape, F32), chip_array((vhl.shape[0], side, rank), F32)]
    out_specs = [vmem, vmem]
    scratch = [pltpu.VMEM((GROUP, side, side), F32)] + [pltpu.VMEM((GROUP, 2, side, side), BF16)] * 2
    if step == STEPS - 1:
        outs.append(jax.ShapeDtypeStruct(ubase.shape, F32))
        out_specs.append(pl.BlockSpec(memory_space=pl.ANY))
        scratch.append(pltpu.SemaphoreType.DMA((cnt.shape[2],)))
    return pl.pallas_call(
        functools.partial(grads_kernel, step),
        out_shape=tuple(outs),
        in_specs=[smem, smem, vmem, vmem, vmem, vmem],
        out_specs=tuple(out_specs),
        scratch_shapes=scratch,
        input_output_aliases={4: 0},
        compiler_params=pltpu.CompilerParams(vmem_limit_bytes=VMEM_LIMIT),
        name=f"grads{step}",
    )(idx, cnt, on_chip(uhl), on_chip(vhl), on_chip(ubase), on_chip(ratings))


class Links:
    def __init__(self, sends, recvs):
        self.sends, self.recvs = sends, recvs
        self.started = []
        self.count = 0

    def message(self):
        self.count += 1
        return self.count - 1

    def copy(self, number, src, dst, device):
        return pltpu.make_async_remote_copy(
            src_ref=src,
            dst_ref=dst,
            send_sem=self.sends.at[number],
            recv_sem=self.recvs.at[number],
            device_id=device,
            device_id_type=MESH,
        )

    def send(self, number, src, dst, device):
        copy = self.copy(number, src, dst, device)
        copy.start()
        self.started.append(copy)

    def arrived(self, number, dst, device):
        self.copy(number, dst, dst, device).wait_recv()


PARTS = (("X", 0, 48), ("Y", 48, 48), ("Y", 96, 32))
GATHER_ORDER = (
    ("GY", 0, 1),
    ("GX", 1, 0),
    ("GY", 2, 1),
    ("GX", 2, 0),
    ("GX", 0, 0),
    ("GY", 1, 1),
    ("GF", 0, 1),
    ("GY", 1, 0),
    ("GX", 0, 1),
    ("GY", 2, 0),
    ("GX", 0, 2),
    ("GF", 2, 1),
    ("GF", 1, 1),
    ("GF", 1, 0),
    ("GF", 2, 0),
)
FULL_ORDER = (
    ("A", 1, 0),
    ("S", 0, 0),
    ("A", 2, 1),
    ("B", 2, 0),
    ("A", 2, 0),
    ("B", 1, 0),
    ("S", 0, 1),
    ("C", 1, 0),
    ("A", 1, 1),
    ("A", 0, 1),
    ("S", 0, 2),
    ("B", 1, 1),
    ("C", 2, 0),
    ("X", 1),
    ("C", 1, 1),
    ("C", 0, 1),
    ("B", 0, 1),
    ("X", 2),
    ("C", 2, 1),
    ("B", 2, 1),
    ("N", 1),
    ("N", 0),
    ("N", 2),
    ("GY", 1, 1),
    ("GX", 1, 0),
    ("GY", 0, 1),
    ("GX", 2, 0),
    ("GY", 2, 1),
    ("GY", 1, 0),
    ("GX", 0, 0),
    ("GX", 0, 1),
    ("GF", 0, 1),
    ("GY", 2, 0),
    ("GF", 2, 1),
    ("GF", 1, 0),
    ("GF", 1, 1),
    ("GX", 0, 2),
    ("GF", 2, 0),
)
REDUCE_ORDER = (
    ("A", 1, 0),
    ("S", 0, 0),
    ("B", 2, 0),
    ("A", 2, 0),
    ("S", 0, 1),
    ("B", 1, 0),
    ("A", 1, 1),
    ("C", 1, 0),
    ("A", 2, 1),
    ("S", 0, 2),
    ("A", 0, 1),
    ("C", 2, 0),
    ("B", 1, 1),
    ("C", 1, 1),
    ("X", 1),
    ("B", 0, 1),
    ("C", 0, 1),
    ("X", 2),
    ("C", 2, 1),
    ("B", 2, 1),
    ("N", 1),
    ("N", 0),
    ("N", 2),
)


def part_halves(part):
    first, size = part
    return (pl.ds(first, size // 2), pl.ds(first + size // 2, size // 2))


def exchange_kernel(step, reduce, gather, *refs):
    refs = list(refs)
    gv = refs.pop(0) if reduce else None
    vin = refs.pop(0)
    uin, rin_hbm = (refs.pop(0), refs.pop(0)) if gather else (None, None)
    vout = refs.pop(0)
    vhl, uhl, ubase, rout = (refs.pop(0) for _ in range(4)) if gather else (None,) * 4
    if reduce:
        xin, xsum, opp, stage, rin, xio, vnew = (refs.pop(0) for _ in range(7))
    if gather:
        vx, vy, vo = (refs.pop(0) for _ in range(3))
    if gather and not reduce:
        uraw = refs.pop(0)
    if gather:
        load_sems, rate_sem, own_sem = refs.pop(0), refs.pop(0), refs.pop(0)
    sends, recvs = refs

    loads = []
    if gather:
        uwork = uin if reduce else uraw
        rates = pltpu.make_async_copy(rin_hbm.at[step], rout, rate_sem)
        kept = pltpu.make_async_copy(vin, vout, own_sem)

    def start_loads():
        if gather:
            if not reduce:
                kept.start()
                span = uin.shape[0] // LOADS
                for i in range(LOADS):
                    piece = pl.ds(i * span, span)
                    loads.append(pltpu.make_async_copy(uin.at[piece], uraw.at[piece], load_sems.at[i]))
                for load in loads:
                    load.start()
            rates.start()

    blk, user = lax.axis_index("blk"), lax.axis_index("user")
    blks = lax.axis_size("blk")
    y, xl = lax.div(user, 2), lax.rem(user, 2)
    ys = lax.axis_size("user") // 2
    up, down, across = lax.rem(y + 1, ys), lax.rem(y + ys - 1, ys), lax.rem(y + 2, ys)
    near = (up, down)
    to_y = ((blk, up * 2 + xl), (blk, down * 2 + xl))
    from_y = (to_y[1], to_y[0])
    to_x = (blk, y * 2 + 1 - xl)
    after = (lax.rem(blk + 1, blks), user)
    before = (lax.rem(blk + blks - 1, blks), user)

    def number(row, which):
        return row * 2 + (1 - xl if which == 0 else xl)

    side = vin.shape[0]
    kinds = [kind for kind, first, size in PARTS]
    halves = [part_halves((first, size)) for kind, first, size in PARTS]
    whole = [pl.ds(first, size) for kind, first, size in PARTS]
    links = Links(sends, recvs)
    both = (0, 1)

    done = [0]

    def user_work(amount):
        if not gather:
            return
        blocks = uin.shape[0]
        start = done[0]
        stop = min(blocks, start + amount)
        done[0] = stop
        if start == stop:
            return
        while loads and (LOADS - len(loads)) * (blocks // LOADS) < stop:
            loads.pop(0).wait()

        def one(i, carry):
            x = uwork[i]
            hi, lo = split(x)
            uhl[i, :side] = hi
            uhl[i, side:] = lo
            ubase[i] = x * (1.0 - USER_RATE * DECAY)
            return carry

        lax.fori_loop(start, stop, one, 0)

    barrier = pltpu.get_barrier_semaphore()
    greet = [to_y[0], to_y[1], to_x] + ([before] if reduce else [])
    for device in greet:
        pl.semaphore_signal(barrier, inc=1, device_id=device, device_id_type=MESH)
    pl.semaphore_wait(barrier, len(greet))

    ids = {}

    def number_of(*key):
        if key not in ids:
            ids[key] = links.message()
        return ids[key]

    def send(key, src, dst, device):
        links.send(number_of(*key), src, dst, device)

    def arrived(key, dst, device):
        links.arrived(number_of(*key), dst, device)

    def arrived_both(kind, p, w, ref, rows_of):
        for d in both:
            arrived((kind, p, d, w), ref.at[d, w, rows_of(d)], from_y[d])

    own = None
    if gather:
        own = vnew.at[1] if reduce else vin
    roles = (across, up, down, y)


    def send_s(p, r):
        for role in ((0,), (1, 2), (3,))[r]:
            at = whole[p]
            send(("S", p, role), gv.at[number(roles[role], 0), at], xin.at[role, at], to_x)

    def need_s(p, role):
        at = whole[p]
        arrived(("S", p, role), xin.at[role, at], to_x)
        xsum[role, at] = gv[number(roles[role], 1), at] + xin[role, at]

    def ours(p, role, row, w):
        return xsum.at[role] if kinds[p] == "X" else gv.at[number(row, w)]

    def send_a(p, w):
        for d in both:
            at = halves[p][d]
            send(("A", p, d, w), ours(p, 0, across, w).at[at], opp.at[d, w, at], to_y[d])

    def send_b(p, w):
        for d in both:
            at = halves[p][1 - d]
            send(("B", p, d, w), ours(p, 1 + d, near[d], w).at[at], rin.at[d, w, at], to_y[d])

    def send_c(p, w):
        for d in both:
            at = halves[p][d]
            stage[d, w, at] = ours(p, 1 + d, near[d], w)[at] + opp[d, w, at]
            send(("C", p, d, w), stage.at[d, w, at], rin.at[d, w, at], to_y[d])

    def send_x(p):
        at = whole[p]
        xio[0, at] = gv[number(y, 0), at] + (rin[0, 0, at] + rin[1, 0, at])
        send(("X", p), xio.at[0, at], xio.at[1, at], to_x)

    def send_n(p):
        at = whole[p]
        mine = xsum[3, at] if kinds[p] == "X" else gv[number(y, 1), at] + xio[1, at]
        grad = mine + (rin[0, 1, at] + rin[1, 1, at])
        old = vin[at]
        vnew[0, at] = old + ITEM_RATE * (grad - DECAY * old)
        send(("N", p), vnew.at[0, at], vnew.at[1, at], after)

    def send_gx(p, k):
        at = whole[p]
        if k == 0:
            send(("GX", p, 0), own.at[at], vx.at[at], to_x)
        elif k == 1:
            for d in both:
                send(("GX", p, 1 + d), vy.at[d, 1, at], vy.at[d, 0, at], to_x)
        else:
            send(("GX", p, 3), vo.at[1, at], vo.at[0, at], to_x)

    def send_gy(p, w):
        at = whole[p]
        for d in both:
            send(("GY", p, d, w), (own if w else vx).at[at], vy.at[d, w, at], to_y[d])

    def send_gf(p, w):
        for d in both:
            at = halves[p][d]
            send(("GF", p, d, w), vy.at[d, w, at], vo.at[w, at], to_y[d])

    waited = set()

    def need(*key):
        if key in waited:
            return
        waited.add(key)
        kind, p = key[0], key[1]
        at = whole[p]
        if kind == "S":
            for role in ((0,), (1, 2), (3,))[key[2]]:
                need_s(p, role)
        elif kind == "A":
            arrived_both("A", p, key[2], opp, lambda d: halves[p][d])
        elif kind == "B":
            arrived_both("B", p, key[2], rin, lambda d: halves[p][1 - d])
        elif kind == "C":
            arrived_both("C", p, key[2], rin, lambda d: halves[p][d])
        elif kind == "X":
            arrived(("X", p), xio.at[1, at], to_x)
        elif kind == "N":
            arrived(("N", p), vnew.at[1, at], before)
        elif kind == "GX" and key[2] == 0:
            arrived(("GX", p, 0), vx.at[at], to_x)
        elif kind == "GX" and key[2] == 1:
            for d in both:
                arrived(("GX", p, 1 + d), vy.at[d, 0, at], to_x)
        elif kind == "GX":
            arrived(("GX", p, 3), vo.at[0, at], to_x)
        elif kind == "GY":
            arrived_both("GY", p, key[2], vy, lambda d: whole[p])
        elif kind == "GF":
            for d in both:
                arrived(("GF", p, d, key[2]), vo.at[key[2], halves[p][d]], from_y[d])

    def act(kind, p, *rest):
        x_first = kinds[p] == "X"
        if kind == "S":
            send_s(p, *rest)
        elif kind == "A":
            if x_first:
                need("S", p, 0)
            send_a(p, *rest)
        elif kind == "B":
            if x_first:
                need("S", p, 1)
            send_b(p, *rest)
        elif kind == "C":
            need("A", p, *rest)
            if x_first:
                need("S", p, 1)
            send_c(p, *rest)
        elif kind == "X":
            need("B", p, 0)
            need("C", p, 0)
            send_x(p)
        elif kind == "N":
            need("B", p, 1)
            need("C", p, 1)
            need(*(("S", p, 2) if x_first else ("X", p)))
            send_n(p)
        elif kind == "GX":
            if rest[0] == 1:
                need("GY", p, 1)
            elif rest[0] == 2:
                need("GF", p, 1)
            elif reduce:
                need("N", p)
            send_gx(p, *rest)
        elif kind == "GY":
            if rest[0] == 0:
                need("GX", p, 0)
            elif reduce:
                need("N", p)
            send_gy(p, *rest)
        elif kind == "GF":
            need("GY", p, *rest)
            send_gf(p, *rest)

    def divide(block, ref):
        hi, lo = split(ref[...])
        vhl[block, :side] = hi
        vhl[block, side:] = lo

    order = FULL_ORDER if reduce and gather else REDUCE_ORDER if reduce else GATHER_ORDER
    early = 8 if reduce else 5
    for turn, action in enumerate(order):
        act(*action)
        if turn == early:
            start_loads()
        if turn > early:
            user_work(1)
    user_work(64)

    parts = range(len(PARTS))
    if gather:
        if reduce:
            vout[...] = vnew[1]
        else:
            kept.wait()
        divide(user, own if reduce else vout)
        for p in parts:
            need("GX", p, 0)
        divide(number(y, 0), vx)
        for w in (1, 0):
            for p in parts:
                if kinds[p] == "X" and not w:
                    need("GX", p, 1)
                else:
                    need("GY", p, w)
            for d in both:
                divide(number((down, up)[d], w), vy.at[d, w])
        for w in (1, 0):
            for p in parts:
                if kinds[p] == "X" and not w:
                    need("GX", p, 2)
                else:
                    need("GF", p, w)
            divide(number(across, w), vo.at[w])
        rates.wait()
    else:
        for p in parts:
            need("N", p)
        vout[...] = vnew[1]
    for copy in links.started:
        copy.wait_send()


MESSAGES = 128
LOADS = 4


def exchange(which, step, gv, own, users_in, ratings):
    reduce, gather = gv is not None, users_in is not None
    side, rank = own.shape
    vmem = pl.BlockSpec(memory_space=pltpu.VMEM)
    anywhere = pl.BlockSpec(memory_space=pl.ANY)
    args = [on_chip(gv), on_chip(own)] if reduce else [off_chip(own)]
    in_specs = [vmem, vmem] if reduce else [anywhere]
    outs, scratch = [chip_array((side, rank), F32)], []
    if reduce:
        scratch += [
            pltpu.VMEM((4, side, rank), F32),
            pltpu.VMEM((4, side, rank), F32),
            pltpu.VMEM((2, 2, side, rank), F32),
            pltpu.VMEM((2, 2, side, rank), F32),
            pltpu.VMEM((2, 2, side, rank), F32),
            pltpu.VMEM((2, side, rank), F32),
            pltpu.VMEM((2, side, rank), F32),
        ]
    if gather:
        blocks = users_in.shape[0]
        args += [on_chip(users_in) if reduce else off_chip(users_in), off_chip(ratings)]
        in_specs += [vmem if reduce else anywhere, anywhere]
        outs += [
            chip_array((8, 2 * side, rank), BF16),
            chip_array((blocks, 2 * side, rank), BF16),
            chip_array((blocks, side, rank), F32),
            chip_array(ratings.shape[1:], jnp.int32),
        ]
        scratch += [
            pltpu.VMEM((side, rank), F32),
            pltpu.VMEM((2, 2, side, rank), F32),
            pltpu.VMEM((2, side, rank), F32),
        ]
        if not reduce:
            scratch.append(pltpu.VMEM((blocks, side, rank), F32))
        scratch += [pltpu.SemaphoreType.DMA((LOADS,)), pltpu.SemaphoreType.DMA, pltpu.SemaphoreType.DMA]
    scratch += [pltpu.SemaphoreType.DMA((MESSAGES,))] * 2
    return pl.pallas_call(
        functools.partial(exchange_kernel, step, reduce, gather),
        out_shape=tuple(outs),
        in_specs=in_specs,
        out_specs=(vmem,) * len(outs),
        scratch_shapes=scratch,
        compiler_params=pltpu.CompilerParams(
            collective_id=which, has_side_effects=True, vmem_limit_bytes=VMEM_LIMIT
        ),
        name=f"exchange{which}",
    )(*args)


def local(user_factors, item_factors, block_index, block_count, ratings):
    side = ratings.shape[-1]
    rank = user_factors.shape[1]
    users = user_factors.reshape(-1, side, rank)
    flat = ratings.reshape(STEPS, -1, side, side)
    block_index = block_index.transpose(0, 2, 3, 1)
    block_count = block_count.transpose(0, 2, 1)
    own, vhl, uhl, ubase, rates = exchange(0, 0, None, item_factors, users, flat)
    for step in range(STEPS):
        users, gv, *final = local_grads(step, block_index, block_count, uhl, vhl, ubase, rates)
        if step < STEPS - 1:
            own, vhl, uhl, ubase, rates = exchange(step + 1, step + 1, gv, own, users, flat)
        else:
            (own,) = exchange(STEPS, 0, gv, own, None, None)
    return (final[0].reshape(user_factors.shape), own)


def solution(mesh):
    in_specs = (
        P(("blk", "user"), None),
        P(("blk", "user"), None),
        P(None, ("blk", "user"), None, None),
        P(None, ("blk", "user"), None),
        P(None, ("blk", "user"), None, None, None, None),
    )
    out_specs = (P(("blk", "user"), None), P(("blk", "user"), None))
    return jax.shard_map(local, mesh=mesh, in_specs=in_specs, out_specs=out_specs, check_vma=False)
```

```python
import functools

import jax
import jax.numpy as jnp
from jax import lax
from jax.experimental import pallas as pl
from jax.experimental.pallas import tpu as pltpu
from jax.sharding import PartitionSpec as P

STEPS = 3
USER_RATE = 0.01
ITEM_RATE = 0.0015
DECAY = 0.05
MESH = pl.DeviceIdType.MESH
F32 = jnp.float32
BF16 = jnp.bfloat16
GROUP = 4
VMEM_LIMIT = 16 << 20
COPY_IN = False


def split(x):
    hi = x.astype(BF16)
    return hi, (x - hi.astype(F32)).astype(BF16)


def chip_array(shape, dtype):
    return pltpu.VMEM(shape, dtype)


def on_chip(x):
    return pltpu.with_memory_space_constraint(x, pltpu.VMEM)


def off_chip(x):
    return pltpu.with_memory_space_constraint(x, pltpu.HBM)


def matmul(a, b, dims=((1,), (0,))):
    return lax.dot_general(a, b, (dims, ((), ())), preferred_element_type=F32)


def grads_kernel(step, idx, cnt, uhl, vhl, ubase, ratings, unew, gv, *refs):
    final, out_sems = (refs[0], refs[-1]) if step == STEPS - 1 else (None, None)
    psc, rsc, tsc = refs[1:4] if step == STEPS - 1 else refs
    cols, rows = cnt.shape[1], cnt.shape[2]
    tiles = rows * cols
    side = psc.shape[1]
    slots = idx.shape[2]
    sub = uhl.shape[0] // rows
    never = 1 << 20

    total = 0
    for t in range(rows):
        for c in range(cols):
            total = total + cnt[step, c, t]
    groups = lax.div(total + (GROUP - 1), GROUP)

    def locate(tile, slot):
        near = jnp.minimum(tile, tiles - 1)
        t, c = lax.div(near, cols), lax.rem(near, cols)
        q = idx[step, c, slot, t]
        last = slot + 1 >= cnt[step, c, t]
        spot = (t * sub + lax.div(q, sub), c * sub + lax.rem(q, sub), near * slots + slot)
        return spot, jnp.where(last, tile + 1, tile), jnp.where(last, 0, slot + 1)

    def group_at(cursor):
        spots, floors = [], []
        tile, slot = cursor
        for _ in range(GROUP):
            floors.append(jnp.where(tile < tiles, 0, never))
            spot, tile, slot = locate(tile, slot)
            spots += spot
        return (*spots, *floors), (tile, slot)

    def predict(group):
        for g in range(GROUP):
            row, item = group[3 * g], group[3 * g + 1]
            parts = matmul(uhl[row], vhl[item], ((1,), (1,)))
            psc[g] = parts[:side, :side] + (parts[:side, side:] + parts[side:, :side])

    def residual(group, over):
        for g in range(GROUP):
            rating = ratings[group[3 * g + 2]]
            floor = jnp.where(over, never, group[3 * GROUP + g])
            res = jnp.where(rating > floor, 0.5 * rating.astype(F32) - psc[g], 0.0)
            for into, x in ((rsc, res), (tsc, res.T)):
                hi, lo = split(x)
                into[g, 0] = hi
                into[g, 1] = lo

    def product(left, g, right):
        hi, lo = left[g, 0], left[g, 1]
        twice = jnp.concatenate(
            [jnp.concatenate([hi, hi], axis=1), jnp.concatenate([lo, lo], axis=1)], axis=0
        )
        both = matmul(twice, right[...])
        return both[:side] + both[side:]

    def update(group):
        for g in range(GROUP):
            row, item = group[3 * g], group[3 * g + 1]
            unew[row] += USER_RATE * product(rsc, g, vhl.at[item])
            gv[item] += product(tsc, g, uhl.at[row])

    def put(row):
        part = pl.ds(row * sub, sub)
        return pltpu.make_async_copy(unew.at[part], final.at[part], out_sems.at[row])

    def start_put(row, carry):
        put(row).start()
        return carry

    gv[...] = jnp.zeros_like(gv)
    if COPY_IN:
        unew[...] = ubase[...]
    one, cursor = group_at((jnp.int32(0), jnp.int32(0)))
    predict(one)
    residual(one, False)
    two, cursor = group_at(cursor)
    predict(two)

    def body(i, carry):
        now, coming, cursor = carry
        fresh, cursor = group_at(cursor)
        update(now)
        residual(coming, i + 1 >= groups)
        predict(fresh)
        if final is not None:
            here, there = (lax.div(group[2], cols * slots) for group in (now, coming))
            lax.fori_loop(here, jnp.where(i + 1 >= groups, rows, there), start_put, 0)
        return coming, fresh, cursor

    lax.fori_loop(0, groups, body, (one, two, cursor))
    if final is not None:
        for row in range(rows):
            put(row).wait()


def local_grads(step, idx, cnt, uhl, vhl, ubase, ratings):
    side = ratings.shape[-1]
    rank = ubase.shape[-1]
    vmem = pl.BlockSpec(memory_space=pltpu.VMEM)
    smem = pl.BlockSpec(memory_space=pltpu.SMEM)
    outs = [chip_array(ubase.shape, F32), chip_array((vhl.shape[0], side, rank), F32)]
    out_specs = [vmem, vmem]
    scratch = [pltpu.VMEM((GROUP, side, side), F32)] + [pltpu.VMEM((GROUP, 2, side, side), BF16)] * 2
    if step == STEPS - 1:
        outs.append(jax.ShapeDtypeStruct(ubase.shape, F32))
        out_specs.append(pl.BlockSpec(memory_space=pl.ANY))
        scratch.append(pltpu.SemaphoreType.DMA((cnt.shape[2],)))
    return pl.pallas_call(
        functools.partial(grads_kernel, step),
        out_shape=tuple(outs),
        in_specs=[smem, smem, vmem, vmem, vmem, vmem],
        out_specs=tuple(out_specs),
        scratch_shapes=scratch,
        input_output_aliases={4: 0},
        compiler_params=pltpu.CompilerParams(vmem_limit_bytes=VMEM_LIMIT),
        name=f"grads{step}",
    )(idx, cnt, on_chip(uhl), on_chip(vhl), on_chip(ubase), on_chip(ratings))


class Links:
    def __init__(self, sends, recvs):
        self.sends, self.recvs = sends, recvs
        self.started = []
        self.count = 0

    def message(self):
        self.count += 1
        return self.count - 1

    def copy(self, number, src, dst, device):
        return pltpu.make_async_remote_copy(
            src_ref=src,
            dst_ref=dst,
            send_sem=self.sends.at[number],
            recv_sem=self.recvs.at[number],
            device_id=device,
            device_id_type=MESH,
        )

    def send(self, number, src, dst, device):
        copy = self.copy(number, src, dst, device)
        copy.start()
        self.started.append(copy)

    def arrived(self, number, dst, device):
        self.copy(number, dst, dst, device).wait_recv()


PARTS = (("X", 0, 48), ("Y", 48, 48), ("Y", 96, 32))
EARLY = 8
FULL_ORDER = (
    ("A", 1, 0),
    ("S", 0, 0),
    ("A", 2, 1),
    ("B", 2, 0),
    ("A", 2, 0),
    ("B", 1, 0),
    ("S", 0, 1),
    ("C", 1, 0),
    ("A", 1, 1),
    ("A", 0, 1),
    ("S", 0, 2),
    ("B", 1, 1),
    ("C", 2, 0),
    ("X", 1),
    ("C", 1, 1),
    ("C", 0, 1),
    ("B", 0, 1),
    ("X", 2),
    ("C", 2, 1),
    ("B", 2, 1),
    ("N", 1),
    ("N", 0),
    ("N", 2),
    ("GY", 1, 1),
    ("GX", 1, 0),
    ("GY", 0, 1),
    ("GX", 2, 0),
    ("GY", 2, 1),
    ("GY", 1, 0),
    ("GX", 0, 0),
    ("GX", 0, 1),
    ("GF", 0, 1),
    ("GY", 2, 0),
    ("GF", 2, 1),
    ("GF", 1, 0),
    ("GF", 1, 1),
    ("GX", 0, 2),
    ("GF", 2, 0),
)
REDUCE_ORDER = (
    ("A", 1, 0),
    ("S", 0, 0),
    ("B", 2, 0),
    ("A", 2, 0),
    ("S", 0, 1),
    ("B", 1, 0),
    ("A", 1, 1),
    ("C", 1, 0),
    ("A", 2, 1),
    ("S", 0, 2),
    ("A", 0, 1),
    ("C", 2, 0),
    ("B", 1, 1),
    ("C", 1, 1),
    ("X", 1),
    ("B", 0, 1),
    ("C", 0, 1),
    ("X", 2),
    ("C", 2, 1),
    ("B", 2, 1),
    ("N", 1),
    ("N", 0),
    ("N", 2),
)


def part_halves(part):
    first, size = part
    return (pl.ds(first, size // 2), pl.ds(first + size // 2, size // 2))


def exchange_kernel(step, reduce, gather, *refs):
    refs = list(refs)
    gv = refs.pop(0) if reduce else None
    vin = refs.pop(0)
    uin, rin_hbm = (refs.pop(0), refs.pop(0)) if gather else (None, None)
    vout = refs.pop(0)
    vhl, uhl, ubase, rout = (refs.pop(0) for _ in range(4)) if gather else (None,) * 4
    if reduce:
        xin, xsum, opp, stage, rin, xio, vnew = (refs.pop(0) for _ in range(7))
    if gather:
        vx, vy, vo = (refs.pop(0) for _ in range(3))
    if gather and not reduce:
        uraw = refs.pop(0)
    if gather:
        load_sems, rate_sem, own_sem = refs.pop(0), refs.pop(0), refs.pop(0)
    sends, recvs = refs

    loads = []
    if gather:
        uwork = uin if reduce else uraw
        rates = pltpu.make_async_copy(rin_hbm.at[step], rout, rate_sem)
        kept = None if reduce else pltpu.make_async_copy(vin, vout, own_sem)

    def start_loads():
        if gather:
            if not reduce:
                kept.start()
                span = uin.shape[0] // LOADS
                for i in range(LOADS):
                    piece = pl.ds(i * span, span)
                    loads.append(pltpu.make_async_copy(uin.at[piece], uraw.at[piece], load_sems.at[i]))
                for load in loads:
                    load.start()
            rates.start()

    blk, user = lax.axis_index("blk"), lax.axis_index("user")
    blks = lax.axis_size("blk")
    y, xl = lax.div(user, 2), lax.rem(user, 2)
    ys = lax.axis_size("user") // 2
    up, down, across = lax.rem(y + 1, ys), lax.rem(y + ys - 1, ys), lax.rem(y + 2, ys)
    near = (up, down)
    to_y = ((blk, up * 2 + xl), (blk, down * 2 + xl))
    from_y = (to_y[1], to_y[0])
    to_x = (blk, y * 2 + 1 - xl)
    after = (lax.rem(blk + 1, blks), user)
    before = (lax.rem(blk + blks - 1, blks), user)

    def number(row, which):
        return row * 2 + (1 - xl if which == 0 else xl)

    side = vin.shape[0]
    kinds = [kind for kind, first, size in PARTS]
    halves = [part_halves((first, size)) for kind, first, size in PARTS]
    whole = [pl.ds(first, size) for kind, first, size in PARTS]
    links = Links(sends, recvs)
    both = (0, 1)

    done = [0]

    def user_work(amount):
        if not gather:
            return
        blocks = uin.shape[0]
        start = done[0]
        stop = min(blocks, start + amount)
        done[0] = stop
        if start == stop:
            return
        while loads and (LOADS - len(loads)) * (blocks // LOADS) < stop:
            loads.pop(0).wait()

        def one(i, carry):
            x = uwork[i]
            hi, lo = split(x)
            uhl[i, :side] = hi
            uhl[i, side:] = lo
            ubase[i] = x * (1.0 - USER_RATE * DECAY)
            return carry

        lax.fori_loop(start, stop, one, 0)

    barrier = pltpu.get_barrier_semaphore()
    greet = [to_y[0], to_y[1], to_x] + ([before] if reduce else [])
    for device in greet:
        pl.semaphore_signal(barrier, inc=1, device_id=device, device_id_type=MESH)
    pl.semaphore_wait(barrier, len(greet))

    ids = {}

    def number_of(*key):
        if key not in ids:
            ids[key] = links.message()
        return ids[key]

    def send(key, src, dst, device):
        links.send(number_of(*key), src, dst, device)

    def arrived(key, dst, device):
        links.arrived(number_of(*key), dst, device)

    def arrived_both(kind, p, w, ref, rows_of):
        for d in both:
            arrived((kind, p, d, w), ref.at[d, w, rows_of(d)], from_y[d])

    own = vnew.at[1] if reduce else vin
    roles = (across, up, down, y)


    def send_s(p, r):
        for role in ((0,), (1, 2), (3,))[r]:
            at = whole[p]
            send(("S", p, role), gv.at[number(roles[role], 0), at], xin.at[role, at], to_x)

    def need_s(p, role):
        at = whole[p]
        arrived(("S", p, role), xin.at[role, at], to_x)
        xsum[role, at] = gv[number(roles[role], 1), at] + xin[role, at]

    def ours(p, role, row, w):
        return xsum.at[role] if kinds[p] == "X" else gv.at[number(row, w)]

    def send_a(p, w):
        for d in both:
            at = halves[p][d]
            send(("A", p, d, w), ours(p, 0, across, w).at[at], opp.at[d, w, at], to_y[d])

    def send_b(p, w):
        for d in both:
            at = halves[p][1 - d]
            send(("B", p, d, w), ours(p, 1 + d, near[d], w).at[at], rin.at[d, w, at], to_y[d])

    def send_c(p, w):
        for d in both:
            at = halves[p][d]
            stage[d, w, at] = ours(p, 1 + d, near[d], w)[at] + opp[d, w, at]
            send(("C", p, d, w), stage.at[d, w, at], rin.at[d, w, at], to_y[d])

    def send_x(p):
        at = whole[p]
        xio[0, at] = gv[number(y, 0), at] + (rin[0, 0, at] + rin[1, 0, at])
        send(("X", p), xio.at[0, at], xio.at[1, at], to_x)

    def send_n(p):
        at = whole[p]
        mine = xsum[3, at] if kinds[p] == "X" else gv[number(y, 1), at] + xio[1, at]
        grad = mine + (rin[0, 1, at] + rin[1, 1, at])
        old = vin[at]
        vnew[0, at] = old + ITEM_RATE * (grad - DECAY * old)
        send(("N", p), vnew.at[0, at], vnew.at[1, at], after)

    def send_gx(p, k):
        at = whole[p]
        if k == 0:
            send(("GX", p, 0), own.at[at], vx.at[at], to_x)
        elif k == 1:
            for d in both:
                send(("GX", p, 1 + d), vy.at[d, 1, at], vy.at[d, 0, at], to_x)
        else:
            send(("GX", p, 3), vo.at[1, at], vo.at[0, at], to_x)

    def send_gy(p, w):
        at = whole[p]
        for d in both:
            send(("GY", p, d, w), (own if w else vx).at[at], vy.at[d, w, at], to_y[d])

    def send_gf(p, w):
        for d in both:
            at = halves[p][d]
            send(("GF", p, d, w), vy.at[d, w, at], vo.at[w, at], to_y[d])

    waited = set()

    def need(*key):
        if key in waited:
            return
        waited.add(key)
        kind, p = key[0], key[1]
        at = whole[p]
        if kind == "S":
            for role in ((0,), (1, 2), (3,))[key[2]]:
                need_s(p, role)
        elif kind == "A":
            arrived_both("A", p, key[2], opp, lambda d: halves[p][d])
        elif kind == "B":
            arrived_both("B", p, key[2], rin, lambda d: halves[p][1 - d])
        elif kind == "C":
            arrived_both("C", p, key[2], rin, lambda d: halves[p][d])
        elif kind == "X":
            arrived(("X", p), xio.at[1, at], to_x)
        elif kind == "N":
            arrived(("N", p), vnew.at[1, at], before)
        elif kind == "GX" and key[2] == 0:
            arrived(("GX", p, 0), vx.at[at], to_x)
        elif kind == "GX" and key[2] == 1:
            for d in both:
                arrived(("GX", p, 1 + d), vy.at[d, 0, at], to_x)
        elif kind == "GX":
            arrived(("GX", p, 3), vo.at[0, at], to_x)
        elif kind == "GY":
            arrived_both("GY", p, key[2], vy, lambda d: whole[p])
        elif kind == "GF":
            for d in both:
                arrived(("GF", p, d, key[2]), vo.at[key[2], halves[p][d]], from_y[d])

    def act(kind, p, *rest):
        x_first = kinds[p] == "X"
        if kind == "S":
            send_s(p, *rest)
        elif kind == "A":
            if x_first:
                need("S", p, 0)
            send_a(p, *rest)
        elif kind == "B":
            if x_first:
                need("S", p, 1)
            send_b(p, *rest)
        elif kind == "C":
            need("A", p, *rest)
            if x_first:
                need("S", p, 1)
            send_c(p, *rest)
        elif kind == "X":
            need("B", p, 0)
            need("C", p, 0)
            send_x(p)
        elif kind == "N":
            need("B", p, 1)
            need("C", p, 1)
            need(*(("S", p, 2) if x_first else ("X", p)))
            send_n(p)
        elif kind == "GX":
            if rest[0] == 1:
                need("GY", p, 1)
            elif rest[0] == 2:
                need("GF", p, 1)
            elif reduce:
                need("N", p)
            send_gx(p, *rest)
        elif kind == "GY":
            if rest[0] == 0:
                need("GX", p, 0)
            elif reduce:
                need("N", p)
            send_gy(p, *rest)
        elif kind == "GF":
            need("GY", p, *rest)
            send_gf(p, *rest)

    def divide(block, ref):
        hi, lo = split(ref[...])
        vhl[block, :side] = hi
        vhl[block, side:] = lo

    def gather_only():
        two = (pl.ds(0, side // 2), pl.ds(side // 2, side // 2))
        for h in both:
            send(("gx", h), vin.at[two[h]], vx.at[two[h]], to_x)
            for d in (h, 1 - h):
                send(("gy", d, 1, h), vin.at[two[h]], vy.at[d, 1, two[h]], to_y[d])
        start_loads()
        for h in both:
            arrived(("gx", h), vx.at[two[h]], to_x)
            for d in (h, 1 - h):
                send(("gy", d, 0, h), vx.at[two[h]], vy.at[d, 0, two[h]], to_y[d])
        for w in (1, 0):
            for d in both:
                arrived(("gy", d, w, d), vy.at[d, w, two[d]], from_y[d])
                send(("gf", d, w), vy.at[d, w, two[d]], vo.at[w, two[d]], to_y[d])
            if w == 1:
                divide(number(y, 0), vx)
                user_work(6)
        user_work(64)
        kept.wait()
        divide(user, vout)
        for w in (1, 0):
            for d in both:
                arrived(("gy", d, w, 1 - d), vy.at[d, w, two[1 - d]], from_y[d])
                divide(number((down, up)[d], w), vy.at[d, w])
        for w in (1, 0):
            for d in both:
                arrived(("gf", d, w), vo.at[w, two[d]], from_y[d])
            divide(number(across, w), vo.at[w])
        rates.wait()

    def by_parts():
        order = FULL_ORDER if gather else REDUCE_ORDER
        for turn, action in enumerate(order):
            act(*action)
            if turn == EARLY:
                start_loads()
            if turn > EARLY:
                user_work(1)
        user_work(64)

        parts = range(len(PARTS))
        if gather:
            vout[...] = vnew[1]
            divide(user, own)
            for p in parts:
                need("GX", p, 0)
            divide(number(y, 0), vx)
            for w in (1, 0):
                for p in parts:
                    if kinds[p] == "X" and not w:
                        need("GX", p, 1)
                    else:
                        need("GY", p, w)
                for d in both:
                    divide(number((down, up)[d], w), vy.at[d, w])
            for w in (1, 0):
                for p in parts:
                    if kinds[p] == "X" and not w:
                        need("GX", p, 2)
                    else:
                        need("GF", p, w)
                divide(number(across, w), vo.at[w])
            rates.wait()
        else:
            for p in parts:
                need("N", p)
            vout[...] = vnew[1]
    by_parts() if reduce else gather_only()
    for copy in links.started:
        copy.wait_send()


MESSAGES = 128
LOADS = 4


def exchange(which, step, gv, own, users_in, ratings):
    reduce, gather = gv is not None, users_in is not None
    side, rank = own.shape
    vmem = pl.BlockSpec(memory_space=pltpu.VMEM)
    anywhere = pl.BlockSpec(memory_space=pl.ANY)
    args = [on_chip(gv), on_chip(own)] if reduce else [off_chip(own)]
    in_specs = [vmem, vmem] if reduce else [anywhere]
    outs, scratch = [chip_array((side, rank), F32)], []
    if reduce:
        scratch += [
            pltpu.VMEM((4, side, rank), F32),
            pltpu.VMEM((4, side, rank), F32),
            pltpu.VMEM((2, 2, side, rank), F32),
            pltpu.VMEM((2, 2, side, rank), F32),
            pltpu.VMEM((2, 2, side, rank), F32),
            pltpu.VMEM((2, side, rank), F32),
            pltpu.VMEM((2, side, rank), F32),
        ]
    if gather:
        blocks = users_in.shape[0]
        args += [on_chip(users_in) if reduce else off_chip(users_in), off_chip(ratings)]
        in_specs += [vmem if reduce else anywhere, anywhere]
        outs += [
            chip_array((8, 2 * side, rank), BF16),
            chip_array((blocks, 2 * side, rank), BF16),
            chip_array((blocks, side, rank), F32),
            chip_array(ratings.shape[1:], jnp.int32),
        ]
        scratch += [
            pltpu.VMEM((side, rank), F32),
            pltpu.VMEM((2, 2, side, rank), F32),
            pltpu.VMEM((2, side, rank), F32),
        ]
        if not reduce:
            scratch.append(pltpu.VMEM((blocks, side, rank), F32))
        scratch += [pltpu.SemaphoreType.DMA((LOADS,)), pltpu.SemaphoreType.DMA, pltpu.SemaphoreType.DMA]
    scratch += [pltpu.SemaphoreType.DMA((MESSAGES,))] * 2
    return pl.pallas_call(
        functools.partial(exchange_kernel, step, reduce, gather),
        out_shape=tuple(outs),
        in_specs=in_specs,
        out_specs=(vmem,) * len(outs),
        scratch_shapes=scratch,
        compiler_params=pltpu.CompilerParams(
            collective_id=which, has_side_effects=True, vmem_limit_bytes=VMEM_LIMIT
        ),
        name=f"exchange{which}",
    )(*args)


def local(user_factors, item_factors, block_index, block_count, ratings):
    side = ratings.shape[-1]
    rank = user_factors.shape[1]
    users = user_factors.reshape(-1, side, rank)
    flat = ratings.reshape(STEPS, -1, side, side)
    block_index = block_index.transpose(0, 2, 3, 1)
    block_count = block_count.transpose(0, 2, 1)
    own, vhl, uhl, ubase, rates = exchange(0, 0, None, item_factors, users, flat)
    for step in range(STEPS):
        users, gv, *final = local_grads(step, block_index, block_count, uhl, vhl, ubase, rates)
        if step < STEPS - 1:
            own, vhl, uhl, ubase, rates = exchange(step + 1, step + 1, gv, own, users, flat)
        else:
            (own,) = exchange(STEPS, 0, gv, own, None, None)
    return (final[0].reshape(user_factors.shape), own)


def solution(mesh):
    in_specs = (
        P(("blk", "user"), None),
        P(("blk", "user"), None),
        P(None, ("blk", "user"), None, None),
        P(None, ("blk", "user"), None),
        P(None, ("blk", "user"), None, None, None, None),
    )
    out_specs = (P(("blk", "user"), None), P(("blk", "user"), None))
    return jax.shard_map(local, mesh=mesh, in_specs=in_specs, out_specs=out_specs, check_vma=False)
```
